512 devices in a mesh: leaf: 8 (over x, core), row: 8 (over y, z_hi), col: 8 (over z_lo).
Axes of the slice: x: 4, y: 4, z: 16 (z_hi: 2, z_lo: 8; z = z_hi * 8 + z_lo), core: 2. Of those that a mesh axis runs over, the one named last changes fastest.
Arguments:
- child_front: float32 [8, 4096, 4096], P('leaf', 'row', 'col'), as said below
- parent_front: bfloat16 [8192, 32768], P('row', ('leaf', 'col')), as said below
- block_map: int32 [8, 30], replicated, may hold values from 0 to 63, as said below
Outputs:
- child_panel_t: float32 [8, 256, 4096], P('leaf', 'col', 'row')
- parent_panel_t: float32 [1024, 8192], P(('leaf', 'col'), 'row')
- parent_update: float32 [8192, 32768], P('row', ('leaf', 'col'))
The draws below stay inside these ranges and needn't reach their ends.
Inputs may be any that keep to these rules, and one draw needn't show every extreme that they name: `child_front`: every child front is symmetric positive definite. `parent_front`: every parent front (each block of 8192 columns) is symmetric positive definite. `block_map`: in each row the entries are distinct. Of the contribution blocks that one device of a child's grid holds in its rows, at most 1 go to parent blocks whose rows one index of row holds; of those it holds in its columns, at most 1 go to parent blocks whose columns are held by one index of col, counting both leaves of the pair together; of all contribution blocks of one child, at most 4 go to parent blocks whose rows one index of row holds. All three bounds are reached.
All inputs are finite; a program needn't handle non-finite values.
Results may differ from the reference program's by a relative error of at most 0.0003.
Values sent between devices are 32-bit elements; how exact they have to be, the bound alone decides.
No kernel may reach another device: no remote copies, remote signals or barrier semaphores. Data moves between devices by JAX's collectives and lax.ppermute only.
A program may use at most 64 MiB of HBM per device.

```python
import jax
import jax.numpy as jnp
from jax import lax

NC = 4096
NP = 8192
BLK = 128
PBC = 256
PBP = 256
CB = 30
PRB = 64
PARENT_COL_BLOCKS = 4
PARENTS = 4
N_LEAF = 8
N_ROW = 8
N_COL = 8


def symmetric_stack(key, copies, order):
    shape = (copies, order, order)
    random_part = jnp.clip(jax.random.normal(key, shape, jnp.float32), -4.0, 4.0)
    symmetric = (random_part + jnp.swapaxes(random_part, 1, 2)) * (0.7071 * order ** (-0.25))
    diagonal = jax.random.uniform(jax.random.fold_in(key, 7), (copies, order, 1), jnp.float32, 2.3, 3.0) * order ** 0.25
    on_diagonal = jnp.arange(order)[:, None] == jnp.arange(order)[None, :]
    return jnp.where(on_diagonal[None], diagonal, symmetric)


def draw_child_front(key, part):
    return symmetric_stack(key, N_LEAF, NC)


def draw_parent_front(key, part):
    stacked = symmetric_stack(key, PARENTS, NP)
    return jnp.transpose(stacked, (1, 0, 2)).reshape(NP, PARENTS * NP).astype(jnp.bfloat16)


def draw_block_map(key, part):
    slope = 2 * N_COL // N_ROW
    block_ids = jnp.arange(CB)
    shift = jax.random.randint(jax.random.fold_in(key, 11), (N_LEAF, 1), 0, 2 * N_COL)
    holding_device = ((slope * block_ids + slope * block_ids // (2 * N_COL))[None, :] + shift) % (2 * N_COL)
    same_owner = holding_device[:, :, None] == holding_device[:, None, :]
    earlier = block_ids[None, :] < block_ids[:, None]
    device_number = jnp.sum(same_owner & earlier[None], axis=2)
    start_positions = jax.random.randint(jax.random.fold_in(key, 13), (N_LEAF, 2 * N_COL), 0, PARENT_COL_BLOCKS)
    selected_entries = jnp.sum(start_positions[:, None, :] * (holding_device[:, :, None] == jnp.arange(2 * N_COL)[None, None, :]), axis=2)
    return (holding_device * PARENT_COL_BLOCKS + (device_number + selected_entries) % PARENT_COL_BLOCKS).astype(jnp.int32)


def setup_inputs(seed: int = 0) -> dict:
    seeds = jax.random.split(jax.random.key(seed), 4)
    return {
        "child_front": draw_child_front(jax.random.fold_in(seeds[3], 71), 0),
        "parent_front": draw_parent_front(jax.random.fold_in(seeds[3], 71), 0),
        "block_map": draw_block_map(jax.random.fold_in(seeds[3], 71), 0),
    }


def factor(front_matrix, panel_width):
    lower_factor = jnp.linalg.cholesky(front_matrix[:panel_width, :panel_width])
    panel_factor = jax.scipy.linalg.solve_triangular(lower_factor, front_matrix[:, :panel_width].T, lower=True).T
    update = jnp.dot(panel_factor, panel_factor.T, precision=lax.Precision.HIGHEST)
    index_ids = jnp.arange(front_matrix.shape[0])
    keep_mask = (index_ids[:, None] >= panel_width) & (index_ids[None, :] >= panel_width)
    return (panel_factor, jnp.where(keep_mask, front_matrix - update, jnp.float32(0.0)))

def reference(child_front, parent_front, block_map):
    child_panels = []
    tile_sets = []
    for child in range(N_LEAF):
        panel_factor, schur_part = factor(child_front[child], PBC)
        child_panels.append(panel_factor.T)
        blocks = schur_part[PBC:, PBC:].reshape(CB, BLK, CB, BLK).transpose(0, 2, 1, 3)
        tile_sets.append(blocks)
    parent_panels = []
    updates = []
    for parent in range(PARENTS):
        front_matrix = parent_front[:, parent * NP:(parent + 1) * NP].astype(jnp.float32)
        tile_grid = front_matrix.reshape(PRB, BLK, PRB, BLK).transpose(0, 2, 1, 3)
        for child in (2 * parent, 2 * parent + 1):
            mapping = block_map[child].astype(jnp.int32)
            tile_grid = tile_grid.at[mapping[:, None], mapping[None, :]].add(tile_sets[child])
        assembled = tile_grid.transpose(0, 2, 1, 3).reshape(NP, NP)
        panel_factor, schur_part = factor(assembled, PBP)
        parent_panels.append(panel_factor.T)
        updates.append(schur_part)
    return (jnp.stack(child_panels), jnp.concatenate(parent_panels, axis=0), jnp.concatenate(updates, axis=1))
```

```python
import functools

import jax
import jax.numpy as jnp
from jax import lax
from jax.experimental import pallas as pl
from jax.experimental.pallas import tpu as pltpu
from jax.sharding import PartitionSpec as P

BLK = 128
STEP = 32
HIGHEST = lax.Precision.HIGHEST


def send(value, axes, pairs):
    return lax.ppermute(value, axes, pairs)


def tree(value, axis, rounds):
    index = lax.axis_index(axis)
    for pairs in rounds:
        got = send(value, axis, pairs)
        is_target = functools.reduce(jnp.logical_or, [index == t for _, t in pairs])
        value = jnp.where(is_target, got, value)
    return value


HALVING = ([(0, 4)], [(0, 2), (4, 6)], [(0, 1), (2, 3), (4, 5), (6, 7)])


def inverse_factor_kernel(a_ref, out_ref, x_ref):
    order = a_ref.shape[0]
    x_ref[...] = a_ref[...]
    for start in range(0, order, STEP):
        stop = start + STEP
        rows = x_ref[start:stop, :]
        block = x_ref[start:stop, start:stop]
        sub = lax.broadcasted_iota(jnp.int32, (STEP, STEP), 0)
        lane = lax.broadcasted_iota(jnp.int32, (STEP, STEP), 1)
        eye = (sub == lane).astype(jnp.float32)
        work = jnp.concatenate([block, eye], axis=1)
        down = lax.broadcasted_iota(jnp.int32, (STEP, 1), 0)
        for k in range(STEP):
            row = work[k : k + 1, :]
            scaled = row / work[k : k + 1, k : k + 1]
            col = jnp.where(down > k, work[:, k : k + 1], 0.0)
            work = work - col * scaled
        pivots = jnp.sum(work[:, :STEP] * eye, axis=1, keepdims=True)
        inverse = work[:, STEP:] * lax.rsqrt(pivots)
        panel = jnp.dot(inverse, rows, precision=HIGHEST, preferred_element_type=jnp.float32)
        place = lax.broadcasted_iota(jnp.int32, (STEP, order), 1)
        pieces = [inverse]
        if start:
            pieces.insert(0, panel[:, :start])
        if stop < order:
            pieces.append(panel[:, stop:])
        panel = jnp.concatenate(pieces, axis=1)
        x_ref[start:stop, :] = panel
        if stop < order:
            upper = panel[:, stop:]
            change = lax.dot_general(
                upper, panel, (((0,), (0,)), ((), ())),
                precision=HIGHEST, preferred_element_type=jnp.float32,
            )
            old = x_ref[stop:, :]
            at = lax.broadcasted_iota(jnp.int32, old.shape, 1)
            old = jnp.where((at >= start) & (at < stop), 0.0, old)
            x_ref[stop:, :] = old - change
    full = x_ref[...]
    sub = lax.broadcasted_iota(jnp.int32, full.shape, 0)
    lane = lax.broadcasted_iota(jnp.int32, full.shape, 1)
    out_ref[...] = jnp.where(lane <= sub, full, 0.0)


def inverse_factor(block):
    return pl.pallas_call(
        inverse_factor_kernel,
        out_shape=jax.ShapeDtypeStruct(block.shape, jnp.float32),
        scratch_shapes=[pltpu.VMEM(block.shape, jnp.float32)],
        name="inverse_factor",
    )(block)


def smem():
    return pl.BlockSpec(memory_space=pltpu.SMEM)


def vmem():
    return pl.BlockSpec(memory_space=pltpu.VMEM)


def strips_kernel(sizes, ids_ref, map_ref, part_ref, out_ref):
    row_span, first, row_blocks = sizes
    row = ids_ref[1]
    for a in range(row_blocks):
        block = row * row_blocks + a - first

        @pl.when(block >= 0)
        def _():
            target = map_ref[jnp.maximum(block, 0)] // row_span
            out_ref[target] = part_ref[a * BLK : (a + 1) * BLK, :]


def tiles_kernel(sizes, ids_ref, map_ref, got_ref, out_ref):
    row_span, col_span, first, row_blocks, col_blocks, cols, count = sizes
    row, col = ids_ref[1], ids_ref[2]

    def body(k, rank):
        here = map_ref[k] // row_span == row

        @pl.when(here)
        def _():
            source = (k + first) // row_blocks
            slot = jnp.minimum(rank, out_ref.shape[1] - 1)
            for y in range(col_blocks):
                block = col * col_blocks + y - first

                @pl.when(block >= 0)
                def _():
                    target = (map_ref[jnp.maximum(block, 0)] // col_span) % cols
                    out_ref[target, slot] = got_ref[source, :, y * BLK : (y + 1) * BLK]

        return rank + here.astype(jnp.int32)

    lax.fori_loop(0, count, body, jnp.int32(0))


def place_kernel(sizes, ids_ref, map_ref, landed_ref, parent_ref, out_ref, other_ref):
    row_span, col_span, first, col_blocks, cols, count = sizes
    half, row, col = ids_ref[0], ids_ref[1], ids_ref[2]
    out_ref[...] = parent_ref[...].astype(jnp.float32)
    other_ref[...] = jnp.zeros_like(other_ref)

    def row_body(k, rank):
        here = map_ref[k] // row_span == row

        @pl.when(here)
        def _():
            slot = jnp.minimum(rank, landed_ref.shape[1] - 1)
            at_row = pl.multiple_of((map_ref[k] % row_span) * BLK, BLK)

            def col_body(j, carry):
                owner = map_ref[j] // col_span
                source = (j + first) // col_blocks
                at = map_ref[j] % col_span

                @pl.when((owner % cols == col) & (owner // cols == half))
                def _():
                    spot = (pl.ds(at_row, BLK), pl.ds(pl.multiple_of(at * BLK, BLK), BLK))
                    out_ref[spot] = out_ref[spot] + landed_ref[source, slot]

                @pl.when((owner % cols == col) & (owner // cols != half))
                def _():
                    other_ref[slot, at] = landed_ref[source, slot]

                return carry

            lax.fori_loop(0, count, col_body, jnp.int32(0))

        return rank + here.astype(jnp.int32)

    lax.fori_loop(0, count, row_body, jnp.int32(0))


def merge_kernel(sizes, ids_ref, map_ref, other_ref, base_ref, out_ref):
    row_span, col_span, count = sizes
    row = ids_ref[1]
    out_ref[...] = base_ref[...]

    def row_body(k, rank):
        here = map_ref[k] // row_span == row

        @pl.when(here)
        def _():
            slot = jnp.minimum(rank, other_ref.shape[0] - 1)
            at_row = pl.multiple_of((map_ref[k] % row_span) * BLK, BLK)
            for at in range(col_span):
                spot = (pl.ds(at_row, BLK), slice(at * BLK, (at + 1) * BLK))
                out_ref[spot] = out_ref[spot] + other_ref[slot, at]

        return rank + here.astype(jnp.int32)

    lax.fori_loop(0, count, row_body, jnp.int32(0))


def shards(child_front, parent_front, block_map):
    leaf_id = lax.axis_index("leaf")
    row_id = lax.axis_index("row")
    col_id = lax.axis_index("col")
    row_count = lax.axis_size("row")
    col_count = lax.axis_size("col")
    leaf_count = lax.axis_size("leaf")
    half_id = leaf_id % 2
    ids = jnp.stack([half_id, row_id, col_id]).astype(jnp.int32)
    own_map = lax.dynamic_index_in_dim(block_map, leaf_id, 0, keepdims=False)
    partner_map = lax.dynamic_index_in_dim(block_map, leaf_id ^ 1, 0, keepdims=False)
    count = own_map.shape[0]

    child_block = child_front[0]
    child_rows, child_cols = child_block.shape
    width = child_cols // 2
    parent_rows, parent_cols = parent_front.shape
    row_span, col_span = parent_rows // BLK, parent_cols // BLK
    row_blocks, col_blocks = child_rows // BLK, child_cols // BLK
    first = width // BLK
    cap = -(-count // row_count)
    swap = [(i, i ^ 1) for i in range(leaf_count)]

    diagonal = child_block[:width, :width]
    spread = [send(diagonal, ("row", "col"), [(0, r * col_count)]) for r in range(1, row_count)]
    diagonal = jnp.where(row_id == 0, diagonal, functools.reduce(jnp.add, spread))
    diagonal = tree(diagonal, "col", HALVING)
    slab = tree(child_block[:, :width], "col", HALVING)
    top = tree(child_block[:width], "row", HALVING)
    inverse = inverse_factor(diagonal)
    rows_factor = lax.dot_general(slab, inverse, (((1,), (1,)), ((), ())), precision=HIGHEST)
    cols_factor = jnp.dot(inverse, top, precision=HIGHEST)
    contribution = child_block - jnp.dot(rows_factor, cols_factor, precision=HIGHEST)
    out_width = width // col_count
    child_out = lax.dynamic_slice_in_dim(rows_factor, col_id * out_width, out_width, 1).T[None]

    strips = pl.pallas_call(
        functools.partial(strips_kernel, (row_span, first, row_blocks)),
        out_shape=jax.ShapeDtypeStruct((row_count, BLK, child_cols), jnp.float32),
        in_specs=[smem(), smem(), vmem()],
        out_specs=vmem(),
        name="strips",
    )(ids, own_map, contribution)
    got = lax.all_to_all(strips, "row", 0, 0, tiled=True)
    tiles = pl.pallas_call(
        functools.partial(
            tiles_kernel, (row_span, col_span, first, row_blocks, col_blocks, col_count, count)
        ),
        out_shape=jax.ShapeDtypeStruct((col_count, cap, BLK, BLK), jnp.float32),
        in_specs=[smem(), smem(), vmem()],
        out_specs=vmem(),
        name="tiles",
    )(ids, own_map, got)
    landed = lax.all_to_all(
        tiles.reshape(col_count, cap * BLK, BLK), "col", 0, 0, tiled=True
    ).reshape(tiles.shape)
    assembled, other = pl.pallas_call(
        functools.partial(place_kernel, (row_span, col_span, first, col_blocks, col_count, count)),
        out_shape=(
            jax.ShapeDtypeStruct(parent_front.shape, jnp.float32),
            jax.ShapeDtypeStruct((cap, col_span, BLK, BLK), jnp.float32),
        ),
        in_specs=[smem(), smem(), vmem(), vmem()],
        out_specs=(vmem(), vmem()),
        name="place",
    )(ids, own_map, landed, parent_front)
    other = send(other.reshape(cap * col_span * BLK, BLK), "leaf", swap).reshape(other.shape)
    assembled = pl.pallas_call(
        functools.partial(merge_kernel, (row_span, col_span, count)),
        out_shape=jax.ShapeDtypeStruct(parent_front.shape, jnp.float32),
        in_specs=[smem(), smem(), vmem(), vmem()],
        out_specs=vmem(),
        name="merge",
    )(ids, partner_map, other, assembled)

    parent_order = parent_rows * row_count
    parent_width = parent_cols // 2
    diagonal = assembled[:parent_width, :parent_width]
    even = range(0, leaf_count, 2)
    grid = row_count * col_count
    spread = [
        send(diagonal, ("leaf", "row", "col"), [(l * grid, l * grid + r * col_count) for l in even])
        for r in range(1, row_count)
    ]
    diagonal = jnp.where(row_id == 0, diagonal, functools.reduce(jnp.add, spread))
    across = [(l, l + 1) for l in even]
    diagonal = jnp.where(half_id == 0, diagonal, send(diagonal, "leaf", across))
    diagonal = tree(diagonal, "col", HALVING)
    slab = assembled[:, :parent_width]
    for pairs in HALVING:
        moves = [(l * col_count + s, l * col_count + t) for l in even for s, t in pairs]
        moved = send(slab, ("leaf", "col"), moves)
        is_target = functools.reduce(jnp.logical_or, [col_id == t for _, t in pairs])
        slab = jnp.where(is_target, moved, slab)
    slab = jnp.where(half_id == 0, slab, send(slab, "leaf", across))
    top = tree(assembled[:parent_width], "row", HALVING)
    inverse = inverse_factor(diagonal)
    rows_factor = lax.dot_general(slab, inverse, (((1,), (1,)), ((), ())), precision=HIGHEST)
    cols_factor = jnp.dot(inverse, top, precision=HIGHEST)
    update = jnp.dot(rows_factor, cols_factor, precision=HIGHEST)
    row_ids = row_id * parent_rows + jnp.arange(parent_rows)
    col_ids = half_id * (parent_order // 2) + col_id * parent_cols + jnp.arange(parent_cols)
    keep = (row_ids[:, None] >= parent_width) & (col_ids[None, :] >= parent_width)
    parent_schur = jnp.where(keep, assembled - update, jnp.float32(0.0))
    share = parent_width // (2 * col_count)
    start = (half_id * col_count + col_id) * share
    parent_out = lax.dynamic_slice_in_dim(rows_factor, start, share, 1).T
    return (child_out, parent_out, parent_schur)


def solution(mesh):
    placed = (P("leaf", "row", "col"), P("row", ("leaf", "col")), P())
    return jax.shard_map(
        shards,
        mesh=mesh,
        in_specs=placed,
        out_specs=(P("leaf", "col", "row"), P(("leaf", "col"), "row"), P("row", ("leaf", "col"))),
        check_vma=False,
    )
```

```python
import functools

import jax
import jax.numpy as jnp
from jax import lax
from jax.experimental import pallas as pl
from jax.experimental.pallas import tpu as pltpu
from jax.sharding import PartitionSpec as P

BLK = 128
STEP = 64
GROUP = 8
HIGHEST = lax.Precision.HIGHEST


def send(value, axes, pairs):
    return lax.ppermute(value, axes, pairs)


def tree(value, axis, rounds):
    index = lax.axis_index(axis)
    for pairs in rounds:
        got = send(value, axis, pairs)
        is_target = functools.reduce(jnp.logical_or, [index == t for _, t in pairs])
        value = jnp.where(is_target, got, value)
    return value


HALVING = ([(0, 4)], [(0, 2), (4, 6)], [(0, 1), (2, 3), (4, 5), (6, 7)])


def reciprocal(x):
    guess = pltpu.reciprocal(x, approx=True)
    guess = guess * (2.0 - x * guess)
    return guess * (2.0 - x * guess)


def inverse_factor_kernel(a_ref, out_ref, x_ref):
    order = a_ref.shape[0]
    f32 = jnp.float32
    value = a_ref[...]
    full_sub = lax.broadcasted_iota(jnp.int32, value.shape, 0)
    full_lane = lax.broadcasted_iota(jnp.int32, value.shape, 1)
    diagonal = jnp.where(full_sub == full_lane, value, 0.0)
    scale_col = lax.rsqrt(jnp.sum(diagonal, axis=1, keepdims=True))
    scale_row = lax.rsqrt(jnp.sum(diagonal, axis=0, keepdims=True))
    x_ref[...] = (value * scale_col) * scale_row
    wide = (STEP, 2 * STEP)
    sub = lax.broadcasted_iota(jnp.int32, wide, 0)
    lane = lax.broadcasted_iota(jnp.int32, wide, 1)
    eye = (sub[:, :STEP] == lane[:, :STEP]).astype(f32)
    for start in range(0, order, STEP):
        stop = start + STEP
        rows = x_ref[start:stop, :]
        work = jnp.concatenate([x_ref[start:stop, start:stop], eye], axis=1)
        for base in range(0, STEP, GROUP):
            cols = [
                jnp.broadcast_to(work[:, base + j : base + j + 1], wide) for j in range(GROUP)
            ]
            for j in range(0, GROUP, 2):
                k = base + j
                c0, c1 = cols[j], cols[j + 1]
                p00, p01, p11 = c0[k : k + 1], c1[k : k + 1], c1[k + 1 : k + 2]
                over = reciprocal(p00 * p11 - p01 * p01)
                a00, a01, a11 = p00 * over, p01 * over, p11 * over
                below = sub > k + 1
                f0 = jnp.where(below, c0 * a11 - c1 * a01, 0.0)
                f1 = jnp.where(below, c1 * a00 - c0 * a01, 0.0)
                for i in range(j + 2, GROUP):
                    cols[i] = cols[i] - f0 * cols[i][k : k + 1] - f1 * cols[i][k + 1 : k + 2]
                work = work - f0 * work[k : k + 1] - f1 * work[k + 1 : k + 2]
        pivots = jnp.sum(jnp.where(sub == lane, work, 0.0), axis=1, keepdims=True)
        left = jnp.sum(jnp.where(sub == lane + 1, work, 0.0), axis=1, keepdims=True)
        above = pltpu.roll(jnp.broadcast_to(pivots, wide), 1, 0)
        work = work - jnp.where(sub % 2 == 1, left / above, 0.0) * pltpu.roll(work, 1, 0)
        pivots = jnp.sum(jnp.where(sub == lane, work, 0.0), axis=1, keepdims=True)
        inverse = work[:, STEP:] * lax.rsqrt(pivots)
        panel = jnp.dot(inverse, rows, precision=HIGHEST, preferred_element_type=f32)
        pieces = [inverse]
        if start:
            pieces.insert(0, panel[:, :start])
        if stop < order:
            pieces.append(panel[:, stop:])
        panel = jnp.concatenate(pieces, axis=1)
        x_ref[start:stop, :] = panel
        if stop < order:
            change = lax.dot_general(
                panel[:, stop:], panel, (((0,), (0,)), ((), ())),
                precision=HIGHEST, preferred_element_type=f32,
            )
            old = x_ref[stop:, :]
            at = lax.broadcasted_iota(jnp.int32, old.shape, 1)
            x_ref[stop:, :] = jnp.where((at >= start) & (at < stop), 0.0, old) - change
    out_ref[...] = jnp.where(full_lane <= full_sub, x_ref[...] * scale_row, 0.0)


def inverse_factor(block):
    return pl.pallas_call(
        inverse_factor_kernel,
        out_shape=jax.ShapeDtypeStruct(block.shape, jnp.float32),
        scratch_shapes=[pltpu.VMEM(block.shape, jnp.float32)],
        name="inverse_factor",
    )(block)


def smem():
    return pl.BlockSpec(memory_space=pltpu.SMEM)


def vmem():
    return pl.BlockSpec(memory_space=pltpu.VMEM)


def row_tables(map_ref, row, row_span, count, rank_ref, at_ref):
    for m in range(at_ref.shape[0]):
        at_ref[m] = -1

    def body(k, rank):
        here = map_ref[k] // row_span == row
        rank_ref[k] = jnp.where(here, rank, -1)

        @pl.when(here)
        def _():
            at_ref[jnp.minimum(rank, at_ref.shape[0] - 1)] = map_ref[k] % row_span

        return rank + here.astype(jnp.int32)

    lax.fori_loop(0, count, body, jnp.int32(0))


def strips_kernel(sizes, ids_ref, map_ref, part_ref, *refs):
    row_span, first, row_blocks, rows = sizes
    outs, slots_ref = refs[:rows], refs[rows]
    row = ids_ref[1]
    for a in range(row_blocks):
        block = row * row_blocks + a - first

        @pl.when(block >= 0)
        def _():
            target = map_ref[jnp.maximum(block, 0)] // row_span
            slots_ref[(target - row + rows) % rows] = part_ref[a * BLK : (a + 1) * BLK, :]

    for s in range(rows):
        outs[s][...] = slots_ref[s]


def tiles_kernel(sizes, ids_ref, map_ref, *refs):
    row_span, col_span, first, row_blocks, col_blocks, rows, cols, count = sizes
    gots, outs = refs[:rows], refs[rows : rows + cols]
    slots_ref, rank_ref, at_ref = refs[rows + cols :]
    row, col = ids_ref[1], ids_ref[2]
    row_tables(map_ref, row, row_span, count, rank_ref, at_ref)
    for s in range(rows):
        source = (row - s + rows) % rows

        def body(a, carry):
            block = source * row_blocks + a - first
            rank = jnp.where(block >= 0, rank_ref[jnp.maximum(block, 0)], -1)

            @pl.when(rank >= 0)
            def _():
                held = gots[s]
                slot = jnp.minimum(rank, slots_ref.shape[1] - 1)
                for y in range(col_blocks):
                    block = col * col_blocks + y - first

                    @pl.when(block >= 0)
                    def _():
                        target = (map_ref[jnp.maximum(block, 0)] // col_span) % cols
                        slots_ref[(target - col + cols) % cols, slot] = held[
                            :, y * BLK : (y + 1) * BLK
                        ]

            return carry

        lax.fori_loop(0, row_blocks, body, jnp.int32(0))
    for t in range(cols):
        outs[t][...] = slots_ref[t]


def other_kernel(sizes, ids_ref, map_ref, *refs):
    col_span, first, col_blocks, cols = sizes
    gots, out_ref = refs[:cols], refs[cols]
    half, col = ids_ref[0], ids_ref[2]
    out_ref[...] = jnp.zeros_like(out_ref)
    for t in range(cols):
        source = (col - t + cols) % cols

        def body(y, carry):
            block = source * col_blocks + y - first
            spot = map_ref[jnp.maximum(block, 0)]
            owner = spot // col_span

            @pl.when((block >= 0) & (owner % cols == col) & (owner // cols != half))
            def _():
                out_ref[spot % col_span] = gots[t][...]

            return carry

        lax.fori_loop(0, col_blocks, body, jnp.int32(0))


def assemble_kernel(sizes, ids_ref, map_ref, pair_map_ref, parent_ref, own_ref, pair_ref,
                    other_ref, *refs):
    row_span, col_span, first, col_blocks, cols, count = sizes
    gots, out_ref = refs[:cols], refs[cols]
    rank_ref, at_ref, pair_at_ref = refs[cols + 1 :]
    half, row, col = ids_ref[0], ids_ref[1], ids_ref[2]
    out_ref[...] = parent_ref[...].astype(jnp.float32)
    row_tables(pair_map_ref, row, row_span, count, rank_ref, pair_at_ref)
    row_tables(map_ref, row, row_span, count, rank_ref, at_ref)
    caps = at_ref.shape[0]
    for m in range(caps):
        for table, product in ((at_ref, own_ref), (pair_at_ref, pair_ref)):
            at = table[m]

            @pl.when(at >= 0)
            def _():
                spot = (pl.ds(pl.multiple_of(at * BLK, BLK), BLK), slice(None))
                out_ref[spot] = out_ref[spot] - product[m * BLK : (m + 1) * BLK, :]

        at = pair_at_ref[m]

        @pl.when(at >= 0)
        def _():
            for y in range(col_span):
                spot = (
                    pl.ds(pl.multiple_of(at * BLK, BLK), BLK), slice(y * BLK, (y + 1) * BLK)
                )
                out_ref[spot] = out_ref[spot] + other_ref[y, m]

    for t in range(cols):
        source = (col - t + cols) % cols

        def body(y, carry):
            block = source * col_blocks + y - first
            place = map_ref[jnp.maximum(block, 0)]
            owner = place // col_span

            @pl.when((block >= 0) & (owner % cols == col) & (owner // cols == half))
            def _():
                at_col = pl.ds(pl.multiple_of((place % col_span) * BLK, BLK), BLK)
                for m in range(caps):
                    at = at_ref[m]

                    @pl.when(at >= 0)
                    def _():
                        spot = (pl.ds(pl.multiple_of(at * BLK, BLK), BLK), at_col)
                        out_ref[spot] = out_ref[spot] + gots[t][m]

            return carry

        lax.fori_loop(0, col_blocks, body, jnp.int32(0))


def row_slots_kernel(sizes, ids_ref, map_ref, part_ref, out_ref):
    row_span, first, row_blocks = sizes
    row = ids_ref[1]
    for a in range(row_blocks):
        block = row * row_blocks + a - first

        @pl.when(block >= 0)
        def _():
            target = map_ref[jnp.maximum(block, 0)] // row_span
            out_ref[target] = part_ref[:, a * BLK : (a + 1) * BLK]


def col_slots_kernel(sizes, ids_ref, map_ref, part_ref, out_ref):
    col_span, first, col_blocks, cols = sizes
    col = ids_ref[2]
    for y in range(col_blocks):
        block = col * col_blocks + y - first

        @pl.when(block >= 0)
        def _():
            target = (map_ref[jnp.maximum(block, 0)] // col_span) % cols
            out_ref[target] = part_ref[:, y * BLK : (y + 1) * BLK]


def row_pick_kernel(sizes, ids_ref, map_ref, got_ref, out_ref, rank_ref, at_ref):
    row_span, first, row_blocks, count = sizes
    row_tables(map_ref, ids_ref[1], row_span, count, rank_ref, at_ref)
    out_ref[...] = jnp.zeros_like(out_ref)

    def body(k, carry):
        rank = rank_ref[k]

        @pl.when(rank >= 0)
        def _():
            out_ref[jnp.minimum(rank, out_ref.shape[0] - 1)] = got_ref[(k + first) // row_blocks]

        return carry

    lax.fori_loop(0, count, body, jnp.int32(0))


def col_pick_kernel(sizes, ids_ref, map_ref, got_ref, own_ref, other_ref):
    col_span, first, col_blocks, cols, count = sizes
    half, col = ids_ref[0], ids_ref[2]
    own_ref[...] = jnp.zeros_like(own_ref)
    other_ref[...] = jnp.zeros_like(other_ref)

    def body(k, carry):
        owner = map_ref[k] // col_span
        for target, wanted in ((own_ref, half), (other_ref, 1 - half)):

            @pl.when((owner % cols == col) & (owner // cols == wanted))
            def _():
                target[map_ref[k] % col_span] = got_ref[(k + first) // col_blocks]

        return carry

    lax.fori_loop(0, count, body, jnp.int32(0))


def kernel_call(body, name, outs, n_smem, n_vmem, scratch=()):
    many = isinstance(outs, list)
    shapes = [jax.ShapeDtypeStruct(o, jnp.float32) for o in (outs if many else [outs])]
    specs = [vmem() for _ in shapes]
    return pl.pallas_call(
        body,
        out_shape=shapes if many else shapes[0],
        in_specs=[smem()] * n_smem + [vmem()] * n_vmem,
        out_specs=specs if many else specs[0],
        scratch_shapes=list(scratch),
        compiler_params=pltpu.CompilerParams(vmem_limit_bytes=40 * 2**20),
        name=name,
    )


def gather_doubling(value, axis, order):
    index = lax.axis_index(axis)
    size = lax.axis_size(axis)
    value = value[None]
    done = []
    for bit in order:
        got = send(value, axis, [(i, i ^ (1 << bit)) for i in range(size)])
        upper = (index >> bit) & 1
        low = jnp.where(upper == 0, value, got)
        high = jnp.where(upper == 0, got, value)
        value = jnp.concatenate([low, high], axis=0)
        done.insert(0, bit)
    bits = len(order)
    shape = value.shape[1:]
    value = value.reshape((2,) * bits + shape)
    perm = [done.index(b) for b in range(bits - 1, -1, -1)]
    value = jnp.transpose(value, perm + list(range(bits, bits + len(shape))))
    return value.reshape((size,) + shape)


def shards(child_front, parent_front, block_map):
    leaf_id = lax.axis_index("leaf")
    row_id = lax.axis_index("row")
    col_id = lax.axis_index("col")
    row_count = lax.axis_size("row")
    col_count = lax.axis_size("col")
    leaf_count = lax.axis_size("leaf")
    half_id = leaf_id % 2
    ids = jnp.stack([half_id, row_id, col_id]).astype(jnp.int32)
    own_map = lax.dynamic_index_in_dim(block_map, leaf_id, 0, keepdims=False)
    partner_map = lax.dynamic_index_in_dim(block_map, leaf_id ^ 1, 0, keepdims=False)
    count = own_map.shape[0]

    child_block = child_front[0]
    child_rows, child_cols = child_block.shape
    width = child_cols // 2
    parent_rows, parent_cols = parent_front.shape
    row_span, col_span = parent_rows // BLK, parent_cols // BLK
    row_blocks, col_blocks = child_rows // BLK, child_cols // BLK
    first = width // BLK
    cap = -(-count // row_count)
    swap = [(i, i ^ 1) for i in range(leaf_count)]

    strips = kernel_call(
        functools.partial(strips_kernel, (row_span, first, row_blocks, row_count)),
        "strips", [(BLK, child_cols)] * row_count, 2, 1,
        [pltpu.VMEM((row_count, BLK, child_cols), jnp.float32)],
    )(ids, own_map, child_block)

    diagonal = child_block[:width, :width]
    spread = [send(diagonal, ("row", "col"), [(0, r * col_count)]) for r in range(1, row_count)]
    diagonal = jnp.where(row_id == 0, diagonal, functools.reduce(jnp.add, spread))
    diagonal = tree(diagonal, "col", HALVING)
    slab = tree(child_block[:, :width], "col", HALVING)
    top = tree(child_block[:width], "row", HALVING)

    got = [strips[0]] + [
        send(strips[s], "row", [(i, (i + s) % row_count) for i in range(row_count)])
        for s in range(1, row_count)
    ]
    tables = [pltpu.SMEM((count,), jnp.int32), pltpu.SMEM((cap,), jnp.int32)]
    tiles = kernel_call(
        functools.partial(
            tiles_kernel,
            (row_span, col_span, first, row_blocks, col_blocks, row_count, col_count, count),
        ),
        "tiles", [(cap, BLK, BLK)] * col_count, 2, row_count,
        [pltpu.VMEM((col_count, cap, BLK, BLK), jnp.float32)] + tables,
    )(ids, own_map, *got)
    landed = [tiles[0]] + [
        send(tiles[t], "col", [(i, (i + t) % col_count) for i in range(col_count)])
        for t in range(1, col_count)
    ]

    inverse = inverse_factor(diagonal)
    cols_factor = jnp.dot(inverse, top, precision=HIGHEST)
    out_width = width // col_count
    share = lax.dynamic_slice_in_dim(inverse, col_id * out_width, out_width, 0)
    child_out = lax.dot_general(share, slab, (((1,), (1,)), ((), ())), precision=HIGHEST)
    piece = (out_width, BLK)

    row_slots = kernel_call(
        functools.partial(row_slots_kernel, (row_span, first, row_blocks)),
        "row_slots", (row_count,) + piece, 2, 1,
    )(ids, own_map, child_out)
    row_got = lax.all_to_all(row_slots, "row", 0, 0, tiled=True)
    row_panel = kernel_call(
        functools.partial(row_pick_kernel, (row_span, first, row_blocks, count)),
        "row_pick", (cap,) + piece, 2, 1, tables,
    )(ids, own_map, row_got)
    row_panel = gather_doubling(row_panel, "col", (2, 1, 0))
    row_panel = jnp.transpose(row_panel, (0, 2, 1, 3)).reshape(width, cap * BLK)
    pair_row_panel = send(row_panel, "leaf", swap)

    col_share = lax.dynamic_slice_in_dim(cols_factor, row_id * out_width, out_width, 0)
    col_slots = kernel_call(
        functools.partial(col_slots_kernel, (col_span, first, col_blocks, col_count)),
        "col_slots", (col_count,) + piece, 2, 1,
    )(ids, own_map, col_share)
    col_got = lax.all_to_all(col_slots, "col", 0, 0, tiled=True)
    own_cols, other_cols = kernel_call(
        functools.partial(col_pick_kernel, (col_span, first, col_blocks, col_count, count)),
        "col_pick", [(col_span,) + piece] * 2, 2, 1,
    )(ids, own_map, col_got)
    col_panels = jnp.stack([own_cols, send(other_cols, "leaf", swap)])
    col_panels = gather_doubling(col_panels, "row", (0, 1, 2))
    col_panels = jnp.transpose(col_panels, (1, 0, 3, 2, 4)).reshape(2, width, col_span * BLK)

    def product(rows, cols):
        return lax.dot_general(rows, cols, (((0,), (0,)), ((), ())), precision=HIGHEST)

    own_product = product(row_panel, col_panels[0])
    pair_product = product(pair_row_panel, col_panels[1])

    other = kernel_call(
        functools.partial(other_kernel, (col_span, first, col_blocks, col_count)),
        "other", (col_span, cap, BLK, BLK), 2, col_count,
    )(ids, own_map, *landed)
    other = send(other, "leaf", swap)
    assembled = kernel_call(
        functools.partial(
            assemble_kernel, (row_span, col_span, first, col_blocks, col_count, count)
        ),
        "assemble", parent_front.shape, 3, 4 + col_count,
        tables + [pltpu.SMEM((cap,), jnp.int32)],
    )(ids, own_map, partner_map, parent_front, own_product, pair_product, other, *landed)

    parent_order = parent_rows * row_count
    parent_width = parent_cols // 2
    diagonal = assembled[:parent_width, :parent_width]
    even = range(0, leaf_count, 2)
    grid = row_count * col_count
    spread = [
        send(diagonal, ("leaf", "row", "col"), [(l * grid, l * grid + r * col_count) for l in even])
        for r in range(1, row_count)
    ]
    diagonal = jnp.where(row_id == 0, diagonal, functools.reduce(jnp.add, spread))
    across = [(l, l + 1) for l in even]
    diagonal = jnp.where(half_id == 0, diagonal, send(diagonal, "leaf", across))
    diagonal = tree(diagonal, "col", HALVING)
    slab = assembled[:, :parent_width]
    for pairs in HALVING:
        moves = [(l * col_count + s, l * col_count + t) for l in even for s, t in pairs]
        moved = send(slab, ("leaf", "col"), moves)
        is_target = functools.reduce(jnp.logical_or, [col_id == t for _, t in pairs])
        slab = jnp.where(is_target, moved, slab)
    slab = jnp.where(half_id == 0, slab, send(slab, "leaf", across))
    top = tree(assembled[:parent_width], "row", HALVING)
    inverse = inverse_factor(diagonal)
    rows_factor = lax.dot_general(slab, inverse, (((1,), (1,)), ((), ())), precision=HIGHEST)
    cols_factor = jnp.dot(inverse, top, precision=HIGHEST)
    update = jnp.dot(rows_factor, cols_factor, precision=HIGHEST)
    row_ids = row_id * parent_rows + jnp.arange(parent_rows)
    col_ids = half_id * (parent_order // 2) + col_id * parent_cols + jnp.arange(parent_cols)
    keep = (row_ids[:, None] >= parent_width) & (col_ids[None, :] >= parent_width)
    parent_schur = jnp.where(keep, assembled - update, jnp.float32(0.0))
    share = parent_width // (2 * col_count)
    start = (half_id * col_count + col_id) * share
    parent_out = lax.dynamic_slice_in_dim(rows_factor, start, share, 1).T
    return (child_out[None], parent_out, parent_schur)


def solution(mesh):
    placed = (P("leaf", "row", "col"), P("row", ("leaf", "col")), P())
    return jax.shard_map(
        shards,
        mesh=mesh,
        in_specs=placed,
        out_specs=(P("leaf", "col", "row"), P(("leaf", "col"), "row"), P("row", ("leaf", "col"))),
        check_vma=False,
    )
```

```python
import functools

import jax
import jax.numpy as jnp
from jax import lax
from jax.experimental import pallas as pl
from jax.experimental.pallas import tpu as pltpu
from jax.sharding import PartitionSpec as P

BLK = 128
STEP = 64
GROUP = 8
HIGHEST = lax.Precision.HIGHEST


def send(value, axes, pairs):
    return lax.ppermute(value, axes, pairs)


HALVING = ([(0, 4)], [(0, 2), (4, 6)], [(0, 1), (2, 3), (4, 5), (6, 7)])


def reciprocal(x):
    guess = pltpu.reciprocal(x, approx=True)
    guess = guess * (2.0 - x * guess)
    return guess * (2.0 - x * guess)


def inverse_factor_kernel(a_ref, out_ref, x_ref):
    order = a_ref.shape[0]
    f32 = jnp.float32
    value = a_ref[...]
    full_sub = lax.broadcasted_iota(jnp.int32, value.shape, 0)
    full_lane = lax.broadcasted_iota(jnp.int32, value.shape, 1)
    diagonal = jnp.where(full_sub == full_lane, value, 0.0)
    scale_col = lax.rsqrt(jnp.sum(diagonal, axis=1, keepdims=True))
    scale_row = lax.rsqrt(jnp.sum(diagonal, axis=0, keepdims=True))
    x_ref[...] = (value * scale_col) * scale_row
    wide = (STEP, 2 * STEP)
    sub = lax.broadcasted_iota(jnp.int32, wide, 0)
    lane = lax.broadcasted_iota(jnp.int32, wide, 1)
    eye = (sub[:, :STEP] == lane[:, :STEP]).astype(f32)
    for start in range(0, order, STEP):
        stop = start + STEP
        rows = x_ref[start:stop, :]
        work = jnp.concatenate([x_ref[start:stop, start:stop], eye], axis=1)
        for base in range(0, STEP, GROUP):
            cols = [
                jnp.broadcast_to(work[:, base + j : base + j + 1], wide) for j in range(GROUP)
            ]
            for j in range(0, GROUP, 2):
                k = base + j
                c0, c1 = cols[j], cols[j + 1]
                p00, p01, p11 = c0[k : k + 1], c1[k : k + 1], c1[k + 1 : k + 2]
                over = reciprocal(p00 * p11 - p01 * p01)
                a00, a01, a11 = p00 * over, p01 * over, p11 * over
                below = sub > k + 1
                f0 = jnp.where(below, c0 * a11 - c1 * a01, 0.0)
                f1 = jnp.where(below, c1 * a00 - c0 * a01, 0.0)
                for i in range(j + 2, GROUP):
                    cols[i] = cols[i] - f0 * cols[i][k : k + 1] - f1 * cols[i][k + 1 : k + 2]
                work = work - f0 * work[k : k + 1] - f1 * work[k + 1 : k + 2]
        pivots = jnp.sum(jnp.where(sub == lane, work, 0.0), axis=1, keepdims=True)
        left = jnp.sum(jnp.where(sub == lane + 1, work, 0.0), axis=1, keepdims=True)
        above = pltpu.roll(jnp.broadcast_to(pivots, wide), 1, 0)
        work = work - jnp.where(sub % 2 == 1, left / above, 0.0) * pltpu.roll(work, 1, 0)
        pivots = jnp.sum(jnp.where(sub == lane, work, 0.0), axis=1, keepdims=True)
        inverse = work[:, STEP:] * lax.rsqrt(pivots)
        panel = jnp.dot(inverse, rows, precision=HIGHEST, preferred_element_type=f32)
        pieces = [inverse]
        if start:
            pieces.insert(0, panel[:, :start])
        if stop < order:
            pieces.append(panel[:, stop:])
        panel = jnp.concatenate(pieces, axis=1)
        x_ref[start:stop, :] = panel
        if stop < order:
            change = lax.dot_general(
                panel[:, stop:], panel, (((0,), (0,)), ((), ())),
                precision=HIGHEST, preferred_element_type=f32,
            )
            old = x_ref[stop:, :]
            at = lax.broadcasted_iota(jnp.int32, old.shape, 1)
            x_ref[stop:, :] = jnp.where((at >= start) & (at < stop), 0.0, old) - change
    out_ref[...] = jnp.where(full_lane <= full_sub, x_ref[...] * scale_row, 0.0)


def inverse_factor(block):
    return pl.pallas_call(
        inverse_factor_kernel,
        out_shape=jax.ShapeDtypeStruct(block.shape, jnp.float32),
        scratch_shapes=[pltpu.VMEM(block.shape, jnp.float32)],
        name="inverse_factor",
    )(block)


def smem():
    return pl.BlockSpec(memory_space=pltpu.SMEM)


def vmem():
    return pl.BlockSpec(memory_space=pltpu.VMEM)


def row_tables(map_ref, row, row_span, count, rank_ref, at_ref):
    for m in range(at_ref.shape[0]):
        at_ref[m] = -1

    def body(k, rank):
        here = map_ref[k] // row_span == row
        rank_ref[k] = jnp.where(here, rank, -1)

        @pl.when(here)
        def _():
            at_ref[jnp.minimum(rank, at_ref.shape[0] - 1)] = map_ref[k] % row_span

        return rank + here.astype(jnp.int32)

    lax.fori_loop(0, count, body, jnp.int32(0))


def strips_kernel(sizes, ids_ref, map_ref, part_ref, *refs):
    row_span, first, row_blocks, rows = sizes
    outs, slots_ref = refs[:rows], refs[rows]
    row = ids_ref[1]
    for a in range(row_blocks):
        block = row * row_blocks + a - first

        @pl.when(block >= 0)
        def _():
            target = map_ref[jnp.maximum(block, 0)] // row_span
            slots_ref[(target - row + rows) % rows] = part_ref[a * BLK : (a + 1) * BLK, :]

    for s in range(rows):
        outs[s][...] = slots_ref[s]


def tiles_kernel(sizes, ids_ref, map_ref, *refs):
    row_span, col_span, first, row_blocks, col_blocks, rows, cols, count = sizes
    gots, outs = refs[:rows], refs[rows : rows + cols]
    slots_ref, rank_ref, at_ref = refs[rows + cols :]
    row, col = ids_ref[1], ids_ref[2]
    row_tables(map_ref, row, row_span, count, rank_ref, at_ref)
    for s in range(rows):
        source = (row - s + rows) % rows

        def body(a, carry):
            block = source * row_blocks + a - first
            rank = jnp.where(block >= 0, rank_ref[jnp.maximum(block, 0)], -1)

            @pl.when(rank >= 0)
            def _():
                held = gots[s]
                slot = jnp.minimum(rank, slots_ref.shape[1] - 1)
                for y in range(col_blocks):
                    block = col * col_blocks + y - first

                    @pl.when(block >= 0)
                    def _():
                        target = (map_ref[jnp.maximum(block, 0)] // col_span) % cols
                        slots_ref[(target - col + cols) % cols, slot] = held[
                            :, y * BLK : (y + 1) * BLK
                        ]

            return carry

        lax.fori_loop(0, row_blocks, body, jnp.int32(0))
    for t in range(cols):
        outs[t][...] = slots_ref[t]


def other_kernel(sizes, ids_ref, map_ref, *refs):
    col_span, first, col_blocks, cols = sizes
    gots, out_ref = refs[:cols], refs[cols]
    half, col = ids_ref[0], ids_ref[2]
    out_ref[...] = jnp.zeros_like(out_ref)
    for t in range(cols):
        source = (col - t + cols) % cols

        def body(y, carry):
            block = source * col_blocks + y - first
            spot = map_ref[jnp.maximum(block, 0)]
            owner = spot // col_span

            @pl.when((block >= 0) & (owner % cols == col) & (owner // cols != half))
            def _():
                out_ref[spot % col_span] = gots[t][...]

            return carry

        lax.fori_loop(0, col_blocks, body, jnp.int32(0))


def assemble_kernel(sizes, ids_ref, map_ref, pair_map_ref, parent_ref, own_ref, pair_ref,
                    other_ref, *refs):
    row_span, col_span, first, col_blocks, cols, count = sizes
    gots, out_ref = refs[:cols], refs[cols]
    rank_ref, at_ref, pair_at_ref = refs[cols + 1 :]
    half, row, col = ids_ref[0], ids_ref[1], ids_ref[2]
    out_ref[...] = parent_ref[...].astype(jnp.float32)
    row_tables(pair_map_ref, row, row_span, count, rank_ref, pair_at_ref)
    row_tables(map_ref, row, row_span, count, rank_ref, at_ref)
    caps = at_ref.shape[0]
    for m in range(caps):
        for table, product in ((at_ref, own_ref), (pair_at_ref, pair_ref)):
            at = table[m]

            @pl.when(at >= 0)
            def _():
                spot = (pl.ds(pl.multiple_of(at * BLK, BLK), BLK), slice(None))
                out_ref[spot] = out_ref[spot] - product[m * BLK : (m + 1) * BLK, :]

        at = pair_at_ref[m]

        @pl.when(at >= 0)
        def _():
            for y in range(col_span):
                spot = (
                    pl.ds(pl.multiple_of(at * BLK, BLK), BLK), slice(y * BLK, (y + 1) * BLK)
                )
                out_ref[spot] = out_ref[spot] + other_ref[y, m]

    for t in range(cols):
        source = (col - t + cols) % cols

        def body(y, carry):
            block = source * col_blocks + y - first
            place = map_ref[jnp.maximum(block, 0)]
            owner = place // col_span

            @pl.when((block >= 0) & (owner % cols == col) & (owner // cols == half))
            def _():
                at_col = pl.ds(pl.multiple_of((place % col_span) * BLK, BLK), BLK)
                for m in range(caps):
                    at = at_ref[m]

                    @pl.when(at >= 0)
                    def _():
                        spot = (pl.ds(pl.multiple_of(at * BLK, BLK), BLK), at_col)
                        out_ref[spot] = out_ref[spot] + gots[t][m]

            return carry

        lax.fori_loop(0, col_blocks, body, jnp.int32(0))


def row_slots_kernel(sizes, ids_ref, map_ref, part_ref, out_ref):
    row_span, first, row_blocks = sizes
    row = ids_ref[1]
    for a in range(row_blocks):
        block = row * row_blocks + a - first

        @pl.when(block >= 0)
        def _():
            target = map_ref[jnp.maximum(block, 0)] // row_span
            out_ref[target] = part_ref[:, a * BLK : (a + 1) * BLK]


def col_slots_kernel(sizes, ids_ref, map_ref, part_ref, out_ref):
    col_span, first, col_blocks, cols = sizes
    col = ids_ref[2]
    for y in range(col_blocks):
        block = col * col_blocks + y - first

        @pl.when(block >= 0)
        def _():
            target = (map_ref[jnp.maximum(block, 0)] // col_span) % cols
            out_ref[target] = part_ref[:, y * BLK : (y + 1) * BLK]


def row_pick_kernel(sizes, ids_ref, map_ref, got_ref, out_ref, rank_ref, at_ref):
    row_span, first, row_blocks, count = sizes
    row_tables(map_ref, ids_ref[1], row_span, count, rank_ref, at_ref)
    out_ref[...] = jnp.zeros_like(out_ref)

    def body(k, carry):
        rank = rank_ref[k]

        @pl.when(rank >= 0)
        def _():
            out_ref[jnp.minimum(rank, out_ref.shape[0] - 1)] = got_ref[(k + first) // row_blocks]

        return carry

    lax.fori_loop(0, count, body, jnp.int32(0))


def col_pick_kernel(sizes, ids_ref, map_ref, got_ref, own_ref, other_ref):
    col_span, first, col_blocks, cols, count = sizes
    half, col = ids_ref[0], ids_ref[2]
    own_ref[...] = jnp.zeros_like(own_ref)
    other_ref[...] = jnp.zeros_like(other_ref)

    def body(k, carry):
        owner = map_ref[k] // col_span
        for target, wanted in ((own_ref, half), (other_ref, 1 - half)):

            @pl.when((owner % cols == col) & (owner // cols == wanted))
            def _():
                target[map_ref[k] % col_span] = got_ref[(k + first) // col_blocks]

        return carry

    lax.fori_loop(0, count, body, jnp.int32(0))


def kernel_call(body, name, outs, n_smem, n_vmem, scratch=()):
    many = isinstance(outs, list)
    shapes = [jax.ShapeDtypeStruct(o, jnp.float32) for o in (outs if many else [outs])]
    specs = [vmem() for _ in shapes]
    return pl.pallas_call(
        body,
        out_shape=shapes if many else shapes[0],
        in_specs=[smem()] * n_smem + [vmem()] * n_vmem,
        out_specs=specs if many else specs[0],
        scratch_shapes=list(scratch),
        compiler_params=pltpu.CompilerParams(vmem_limit_bytes=40 * 2**20),
        name=name,
    )


def shards(child_front, parent_front, block_map):
    leaf_id = lax.axis_index("leaf")
    row_id = lax.axis_index("row")
    col_id = lax.axis_index("col")
    row_count = lax.axis_size("row")
    col_count = lax.axis_size("col")
    leaf_count = lax.axis_size("leaf")
    half_id = leaf_id % 2
    ids = jnp.stack([half_id, row_id, col_id]).astype(jnp.int32)
    own_map = lax.dynamic_index_in_dim(block_map, leaf_id, 0, keepdims=False)
    partner_map = lax.dynamic_index_in_dim(block_map, leaf_id ^ 1, 0, keepdims=False)
    count = own_map.shape[0]

    child_block = child_front[0]
    child_rows, child_cols = child_block.shape
    width = child_cols // 2
    parent_rows, parent_cols = parent_front.shape
    row_span, col_span = parent_rows // BLK, parent_cols // BLK
    row_blocks, col_blocks = child_rows // BLK, child_cols // BLK
    first = width // BLK
    cap = -(-count // row_count)
    swap = [(i, i ^ 1) for i in range(leaf_count)]

    bulk = []

    def step(operands, lag=1):
        operands = list(operands)
        if len(bulk) > lag:
            tied = lax.optimization_barrier((operands, bulk[-1 - lag]))
            operands, bulk[-1 - lag] = tied
        else:
            operands = lax.optimization_barrier(operands)
        return operands

    def only(cell, got, value, targets):
        index = lax.axis_index(cell)
        hit = functools.reduce(jnp.logical_or, [index == t for t in targets])
        return jnp.where(hit, got, value)

    strips = kernel_call(
        functools.partial(strips_kernel, (row_span, first, row_blocks, row_count)),
        "strips", [(BLK, child_cols)] * row_count, 2, 1,
        [pltpu.VMEM((row_count, BLK, child_cols), jnp.float32)],
    )(ids, own_map, child_block)
    strips = list(strips)
    row_pairs = [[(i, (i + s) % row_count) for i in range(row_count)] for s in range(row_count)]
    col_pairs = [[(i, (i + t) % col_count) for i in range(col_count)] for t in range(col_count)]

    def by_rows(pairs):
        return [(r * col_count, q * col_count) for r, q in pairs]

    diagonal, slab, top = child_block[:width, :width], child_block[:, :width], child_block[:width]
    for number, pairs in enumerate(HALVING):
        shift = number + 1
        diagonal, slab, top, strips[shift] = step([diagonal, slab, top, strips[shift]])
        bulk.append(send(strips[shift], "row", row_pairs[shift]))
        targets = [t for _, t in pairs]
        diagonal = only("row", send(diagonal, ("row", "col"), by_rows(pairs)), diagonal, targets)
        slab = only("col", send(slab, "col", pairs), slab, targets)
        top = only("row", send(top, "row", pairs), top, targets)
    for number, pairs in enumerate(HALVING):
        shift = number + 4
        diagonal, slab, top, strips[shift] = step([diagonal, slab, top, strips[shift]])
        bulk.append(send(strips[shift], "row", row_pairs[shift]))
        diagonal = only("col", send(diagonal, "col", pairs), diagonal, [t for _, t in pairs])
    diagonal, slab, top, strips[7] = step([diagonal, slab, top, strips[7]])
    bulk.append(send(strips[7], "row", row_pairs[7]))
    inverse = inverse_factor(diagonal)
    cols_factor = jnp.dot(inverse, top, precision=HIGHEST)
    out_width = width // col_count
    share = lax.dynamic_slice_in_dim(inverse, col_id * out_width, out_width, 0)
    child_out = lax.dot_general(share, slab, (((1,), (1,)), ((), ())), precision=HIGHEST)
    piece = (out_width, BLK)
    row_slots = kernel_call(
        functools.partial(row_slots_kernel, (row_span, first, row_blocks)),
        "row_slots", (row_count,) + piece, 2, 1,
    )(ids, own_map, child_out)
    col_share = lax.dynamic_slice_in_dim(cols_factor, row_id * out_width, out_width, 0)
    col_slots = kernel_call(
        functools.partial(col_slots_kernel, (col_span, first, col_blocks, col_count)),
        "col_slots", (col_count,) + piece, 2, 1,
    )(ids, own_map, col_share)
    row_slots, col_slots, got = lax.optimization_barrier((row_slots, col_slots, bulk))
    got = [strips[0]] + list(got)

    tables = [pltpu.SMEM((count,), jnp.int32), pltpu.SMEM((cap,), jnp.int32)]
    tiles = list(kernel_call(
        functools.partial(
            tiles_kernel,
            (row_span, col_span, first, row_blocks, col_blocks, row_count, col_count, count),
        ),
        "tiles", [(cap, BLK, BLK)] * col_count, 2, row_count,
        [pltpu.VMEM((col_count, cap, BLK, BLK), jnp.float32)] + tables,
    )(ids, own_map, *got))
    bulk = []

    tiles[1], tiles[2], row_slots, col_slots = lax.optimization_barrier(
        (tiles[1], tiles[2], row_slots, col_slots)
    )
    bulk.append(send(tiles[1], "col", col_pairs[1]))
    row_got = lax.all_to_all(row_slots, "row", 0, 0, tiled=True)
    tiles[2], col_slots, row_got = lax.optimization_barrier((tiles[2], col_slots, row_got))
    bulk.append(send(tiles[2], "col", col_pairs[2]))
    col_got = lax.all_to_all(col_slots, "col", 0, 0, tiled=True)
    row_panel = kernel_call(
        functools.partial(row_pick_kernel, (row_span, first, row_blocks, count)),
        "row_pick", (cap,) + piece, 2, 1, tables,
    )(ids, own_map, row_got)
    own_cols, other_cols = kernel_call(
        functools.partial(col_pick_kernel, (col_span, first, col_blocks, col_count, count)),
        "col_pick", [(col_span,) + piece] * 2, 2, 1,
    )(ids, own_map, col_got)

    def doubled(value, axis, bit):
        got = send(value, axis, [(i, i ^ (1 << bit)) for i in range(lax.axis_size(axis))])
        upper = (lax.axis_index(axis) >> bit) & 1
        low = jnp.where(upper == 0, value, got)
        high = jnp.where(upper == 0, got, value)
        return jnp.stack([low, high])

    row_panel, other_cols, tiles[3] = step([row_panel, other_cols, tiles[3]])
    bulk.append(send(tiles[3], "col", col_pairs[3]))
    row_panel = doubled(row_panel, "col", 2)
    col_panels = jnp.stack([own_cols, send(other_cols, "leaf", swap)])
    row_panel, col_panels, tiles[4] = step([row_panel, col_panels, tiles[4]])
    bulk.append(send(tiles[4], "col", col_pairs[4]))
    row_panel = doubled(row_panel, "col", 1)
    col_panels = doubled(col_panels, "row", 0)
    row_panel, col_panels, tiles[5] = step([row_panel, col_panels, tiles[5]])
    bulk.append(send(tiles[5], "col", col_pairs[5]))
    row_panel = doubled(row_panel, "col", 0)
    col_panels = doubled(col_panels, "row", 1)
    row_panel, col_panels, tiles[6] = step([row_panel, col_panels, tiles[6]])
    bulk.append(send(tiles[6], "col", col_pairs[6]))
    row_panel = jnp.transpose(row_panel, (2, 1, 0, 4, 3, 5)).reshape(width, cap * BLK)
    pair_row_panel = send(row_panel, "leaf", swap)
    col_panels = doubled(col_panels, "row", 2)
    row_panel, pair_row_panel, col_panels, tiles[7] = step(
        [row_panel, pair_row_panel, col_panels, tiles[7]]
    )
    bulk.append(send(tiles[7], "col", col_pairs[7]))
    col_panels = jnp.transpose(col_panels, (3, 0, 1, 2, 5, 4, 6))
    col_panels = col_panels.reshape(2, width, col_span * BLK)

    def product(rows, cols):
        return lax.dot_general(rows, cols, (((0,), (0,)), ((), ())), precision=HIGHEST)

    own_product = product(row_panel, col_panels[0])
    pair_product = product(pair_row_panel, col_panels[1])
    landed = [tiles[0]] + bulk
    other = kernel_call(
        functools.partial(other_kernel, (col_span, first, col_blocks, col_count)),
        "other", (col_span, cap, BLK, BLK), 2, col_count,
    )(ids, own_map, *landed)
    other = send(other, "leaf", swap)
    assembled = kernel_call(
        functools.partial(
            assemble_kernel, (row_span, col_span, first, col_blocks, col_count, count)
        ),
        "assemble", parent_front.shape, 3, 4 + col_count,
        tables + [pltpu.SMEM((cap,), jnp.int32)],
    )(ids, own_map, partner_map, parent_front, own_product, pair_product, other, *landed)

    parent_order = parent_rows * row_count
    parent_width = parent_cols // 2
    even = range(0, leaf_count, 2)
    grid = row_count * col_count
    across = [(l, l + 1) for l in even]
    diagonal = assembled[:parent_width, :parent_width]
    slab, top = assembled[:, :parent_width], assembled[:parent_width]
    diagonal, slab, top = lax.optimization_barrier((diagonal, slab, top))

    def spread_rows(value, pairs):
        moves = [
            (l * grid + r * col_count, l * grid + q * col_count) for l in even for r, q in pairs
        ]
        return send(value, ("leaf", "row", "col"), moves)

    def spread_cols(value, pairs):
        moves = [(l * col_count + r, l * col_count + q) for l in even for r, q in pairs]
        return only("col", send(value, ("leaf", "col"), moves), value, [q for _, q in pairs])

    def spread_top(value, pairs):
        return only("row", send(value, "row", pairs), value, [q for _, q in pairs])

    fan = [spread_rows(diagonal, [(0, q)]) for q in (2, 4, 6)]
    diagonal = only("row", functools.reduce(jnp.add, fan), diagonal, (2, 4, 6))
    slab = spread_cols(slab, HALVING[0])
    (diagonal,) = lax.optimization_barrier([diagonal])
    zhi = [(0, 1), (2, 3), (4, 5), (6, 7)]
    diagonal = only("row", spread_rows(diagonal, zhi), diagonal, (1, 3, 5, 7))
    top = spread_top(top, HALVING[0])
    diagonal, slab, top = lax.optimization_barrier((diagonal, slab, top))
    diagonal = spread_cols(diagonal, HALVING[0])
    slab = spread_cols(slab, HALVING[1])
    top = spread_top(top, HALVING[1])
    diagonal, slab, top = lax.optimization_barrier((diagonal, slab, top))
    diagonal = spread_cols(diagonal, HALVING[1])
    slab = spread_cols(slab, HALVING[2])
    top = spread_top(top, HALVING[2])
    diagonal, slab = lax.optimization_barrier((diagonal, slab))
    diagonal = spread_cols(diagonal, HALVING[2])
    diagonal = jnp.where(half_id == 0, diagonal, send(diagonal, "leaf", across))
    slab = jnp.where(half_id == 0, slab, send(slab, "leaf", across))
    inverse = inverse_factor(diagonal)
    rows_factor = lax.dot_general(slab, inverse, (((1,), (1,)), ((), ())), precision=HIGHEST)
    cols_factor = jnp.dot(inverse, top, precision=HIGHEST)
    update = jnp.dot(rows_factor, cols_factor, precision=HIGHEST)
    row_ids = row_id * parent_rows + jnp.arange(parent_rows)
    col_ids = half_id * (parent_order // 2) + col_id * parent_cols + jnp.arange(parent_cols)
    keep = (row_ids[:, None] >= parent_width) & (col_ids[None, :] >= parent_width)
    parent_schur = jnp.where(keep, assembled - update, jnp.float32(0.0))
    share = parent_width // (2 * col_count)
    start = (half_id * col_count + col_id) * share
    parent_out = lax.dynamic_slice_in_dim(rows_factor, start, share, 1).T
    return (child_out[None], parent_out, parent_schur)


def solution(mesh):
    placed = (P("leaf", "row", "col"), P("row", ("leaf", "col")), P())
    return jax.shard_map(
        shards,
        mesh=mesh,
        in_specs=placed,
        out_specs=(P("leaf", "col", "row"), P(("leaf", "col"), "row"), P("row", ("leaf", "col"))),
        check_vma=False,
    )
```

```python
import functools

import jax
import jax.numpy as jnp
from jax import lax
from jax.experimental import pallas as pl
from jax.experimental.pallas import tpu as pltpu
from jax.sharding import PartitionSpec as P

BLK = 128
STEP = 64
GROUP = 8
HIGHEST = lax.Precision.HIGHEST


def send(value, axes, pairs):
    return lax.ppermute(value, axes, pairs)


HALVING = ([(0, 4)], [(0, 2), (4, 6)], [(0, 1), (2, 3), (4, 5), (6, 7)])


def reciprocal(x):
    guess = pltpu.reciprocal(x, approx=True)
    guess = guess * (2.0 - x * guess)
    return guess * (2.0 - x * guess)


def inverse_factor_kernel(a_ref, out_ref, x_ref):
    order = a_ref.shape[0]
    f32 = jnp.float32
    value = a_ref[...]
    full_sub = lax.broadcasted_iota(jnp.int32, value.shape, 0)
    full_lane = lax.broadcasted_iota(jnp.int32, value.shape, 1)
    diagonal = jnp.where(full_sub == full_lane, value, 0.0)
    scale_col = lax.rsqrt(jnp.sum(diagonal, axis=1, keepdims=True))
    scale_row = lax.rsqrt(jnp.sum(diagonal, axis=0, keepdims=True))
    x_ref[...] = (value * scale_col) * scale_row
    wide = (STEP, 2 * STEP)
    sub = lax.broadcasted_iota(jnp.int32, wide, 0)
    lane = lax.broadcasted_iota(jnp.int32, wide, 1)
    eye = (sub[:, :STEP] == lane[:, :STEP]).astype(f32)
    for start in range(0, order, STEP):
        stop = start + STEP
        rows = x_ref[start:stop, :]
        work = jnp.concatenate([x_ref[start:stop, start:stop], eye], axis=1)
        for base in range(0, STEP, GROUP):
            cols = [
                jnp.broadcast_to(work[:, base + j : base + j + 1], wide) for j in range(GROUP)
            ]
            for j in range(0, GROUP, 2):
                k = base + j
                c0, c1 = cols[j], cols[j + 1]
                p00, p01, p11 = c0[k : k + 1], c1[k : k + 1], c1[k + 1 : k + 2]
                over = reciprocal(p00 * p11 - p01 * p01)
                a00, a01, a11 = p00 * over, p01 * over, p11 * over
                below = sub > k + 1
                f0 = jnp.where(below, c0 * a11 - c1 * a01, 0.0)
                f1 = jnp.where(below, c1 * a00 - c0 * a01, 0.0)
                for i in range(j + 2, GROUP):
                    cols[i] = cols[i] - f0 * cols[i][k : k + 1] - f1 * cols[i][k + 1 : k + 2]
                work = work - f0 * work[k : k + 1] - f1 * work[k + 1 : k + 2]
        pivots = jnp.sum(jnp.where(sub == lane, work, 0.0), axis=1, keepdims=True)
        left = jnp.sum(jnp.where(sub == lane + 1, work, 0.0), axis=1, keepdims=True)
        above = pltpu.roll(jnp.broadcast_to(pivots, wide), 1, 0)
        work = work - jnp.where(sub % 2 == 1, left / above, 0.0) * pltpu.roll(work, 1, 0)
        pivots = jnp.sum(jnp.where(sub == lane, work, 0.0), axis=1, keepdims=True)
        inverse = work[:, STEP:] * lax.rsqrt(pivots)
        panel = jnp.dot(inverse, rows, precision=HIGHEST, preferred_element_type=f32)
        pieces = [inverse]
        if start:
            pieces.insert(0, panel[:, :start])
        if stop < order:
            pieces.append(panel[:, stop:])
        panel = jnp.concatenate(pieces, axis=1)
        x_ref[start:stop, :] = panel
        if stop < order:
            change = lax.dot_general(
                panel[:, stop:], panel, (((0,), (0,)), ((), ())),
                precision=HIGHEST, preferred_element_type=f32,
            )
            old = x_ref[stop:, :]
            at = lax.broadcasted_iota(jnp.int32, old.shape, 1)
            x_ref[stop:, :] = jnp.where((at >= start) & (at < stop), 0.0, old) - change
    out_ref[...] = jnp.where(full_lane <= full_sub, x_ref[...] * scale_row, 0.0)


def inverse_factor(block):
    return pl.pallas_call(
        inverse_factor_kernel,
        out_shape=jax.ShapeDtypeStruct(block.shape, jnp.float32),
        scratch_shapes=[pltpu.VMEM(block.shape, jnp.float32)],
        name="inverse_factor",
    )(block)


def smem():
    return pl.BlockSpec(memory_space=pltpu.SMEM)


def vmem():
    return pl.BlockSpec(memory_space=pltpu.VMEM)


def row_tables(map_ref, row, row_span, count, rank_ref, at_ref):
    for m in range(at_ref.shape[0]):
        at_ref[m] = -1

    def body(k, rank):
        here = map_ref[k] // row_span == row
        rank_ref[k] = jnp.where(here, rank, -1)

        @pl.when(here)
        def _():
            at_ref[jnp.minimum(rank, at_ref.shape[0] - 1)] = map_ref[k] % row_span

        return rank + here.astype(jnp.int32)

    lax.fori_loop(0, count, body, jnp.int32(0))


def strips_kernel(sizes, ids_ref, map_ref, part_ref, out_ref):
    row_span, first, row_blocks = sizes
    row = ids_ref[1]
    for a in range(row_blocks):
        block = row * row_blocks + a - first

        @pl.when(block >= 0)
        def _():
            target = map_ref[jnp.maximum(block, 0)] // row_span
            out_ref[target] = part_ref[a * BLK : (a + 1) * BLK, :]


def tiles_kernel(sizes, ids_ref, map_ref, got_ref, out_ref, rank_ref, at_ref):
    row_span, col_span, first, row_blocks, col_blocks, cols, count = sizes
    row, col = ids_ref[1], ids_ref[2]
    row_tables(map_ref, row, row_span, count, rank_ref, at_ref)

    def body(k, carry):
        rank = rank_ref[k]

        @pl.when(rank >= 0)
        def _():
            source = (k + first) // row_blocks
            slot = jnp.minimum(rank, out_ref.shape[1] - 1)
            for y in range(col_blocks):
                block = col * col_blocks + y - first

                @pl.when(block >= 0)
                def _():
                    target = (map_ref[jnp.maximum(block, 0)] // col_span) % cols
                    out_ref[target, slot] = got_ref[source, :, y * BLK : (y + 1) * BLK]

        return carry

    lax.fori_loop(0, count, body, jnp.int32(0))


def other_kernel(sizes, ids_ref, map_ref, landed_ref, out_ref):
    col_span, first, col_blocks, cols, count = sizes
    half, col = ids_ref[0], ids_ref[2]
    out_ref[...] = jnp.zeros_like(out_ref)

    def body(k, carry):
        owner = map_ref[k] // col_span

        @pl.when((owner % cols == col) & (owner // cols != half))
        def _():
            out_ref[map_ref[k] % col_span] = landed_ref[(k + first) // col_blocks]

        return carry

    lax.fori_loop(0, count, body, jnp.int32(0))


def assemble_kernel(sizes, ids_ref, map_ref, pair_map_ref, parent_ref, own_ref, pair_ref,
                    other_ref, landed_ref, out_ref, rank_ref, at_ref, pair_at_ref):
    row_span, col_span, first, col_blocks, cols, count = sizes
    half, row, col = ids_ref[0], ids_ref[1], ids_ref[2]
    out_ref[...] = parent_ref[...].astype(jnp.float32)
    row_tables(pair_map_ref, row, row_span, count, rank_ref, pair_at_ref)
    row_tables(map_ref, row, row_span, count, rank_ref, at_ref)
    caps = at_ref.shape[0]
    for m in range(caps):
        for table, product in ((at_ref, own_ref), (pair_at_ref, pair_ref)):
            at = table[m]

            @pl.when(at >= 0)
            def _():
                spot = (pl.ds(pl.multiple_of(at * BLK, BLK), BLK), slice(None))
                out_ref[spot] = out_ref[spot] - product[m * BLK : (m + 1) * BLK, :]

        at = pair_at_ref[m]

        @pl.when(at >= 0)
        def _():
            for y in range(col_span):
                spot = (
                    pl.ds(pl.multiple_of(at * BLK, BLK), BLK), slice(y * BLK, (y + 1) * BLK)
                )
                out_ref[spot] = out_ref[spot] + other_ref[y, m]

    def body(k, carry):
        owner = map_ref[k] // col_span

        @pl.when((owner % cols == col) & (owner // cols == half))
        def _():
            at_col = pl.ds(pl.multiple_of((map_ref[k] % col_span) * BLK, BLK), BLK)
            for m in range(caps):
                at = at_ref[m]

                @pl.when(at >= 0)
                def _():
                    spot = (pl.ds(pl.multiple_of(at * BLK, BLK), BLK), at_col)
                    out_ref[spot] = out_ref[spot] + landed_ref[(k + first) // col_blocks, m]

        return carry

    lax.fori_loop(0, count, body, jnp.int32(0))


def row_slots_kernel(sizes, ids_ref, map_ref, part_ref, out_ref):
    row_span, first, row_blocks = sizes
    row = ids_ref[1]
    for a in range(row_blocks):
        block = row * row_blocks + a - first

        @pl.when(block >= 0)
        def _():
            target = map_ref[jnp.maximum(block, 0)] // row_span
            out_ref[target] = part_ref[:, a * BLK : (a + 1) * BLK]


def col_slots_kernel(sizes, ids_ref, map_ref, part_ref, out_ref):
    col_span, first, col_blocks, cols = sizes
    col = ids_ref[2]
    for y in range(col_blocks):
        block = col * col_blocks + y - first

        @pl.when(block >= 0)
        def _():
            target = (map_ref[jnp.maximum(block, 0)] // col_span) % cols
            out_ref[target] = part_ref[:, y * BLK : (y + 1) * BLK]


def row_pick_kernel(sizes, ids_ref, map_ref, got_ref, out_ref, rank_ref, at_ref):
    row_span, first, row_blocks, count = sizes
    row_tables(map_ref, ids_ref[1], row_span, count, rank_ref, at_ref)
    out_ref[...] = jnp.zeros_like(out_ref)

    def body(k, carry):
        rank = rank_ref[k]

        @pl.when(rank >= 0)
        def _():
            out_ref[jnp.minimum(rank, out_ref.shape[0] - 1)] = got_ref[(k + first) // row_blocks]

        return carry

    lax.fori_loop(0, count, body, jnp.int32(0))


def col_pick_kernel(sizes, ids_ref, map_ref, got_ref, own_ref, other_ref):
    col_span, first, col_blocks, cols, count = sizes
    half, col = ids_ref[0], ids_ref[2]
    own_ref[...] = jnp.zeros_like(own_ref)
    other_ref[...] = jnp.zeros_like(other_ref)

    def body(k, carry):
        owner = map_ref[k] // col_span
        for target, wanted in ((own_ref, half), (other_ref, 1 - half)):

            @pl.when((owner % cols == col) & (owner // cols == wanted))
            def _():
                target[map_ref[k] % col_span] = got_ref[(k + first) // col_blocks]

        return carry

    lax.fori_loop(0, count, body, jnp.int32(0))


def kernel_call(body, name, outs, n_smem, n_vmem, scratch=()):
    many = isinstance(outs, list)
    shapes = [jax.ShapeDtypeStruct(o, jnp.float32) for o in (outs if many else [outs])]
    specs = [vmem() for _ in shapes]
    return pl.pallas_call(
        body,
        out_shape=shapes if many else shapes[0],
        in_specs=[smem()] * n_smem + [vmem()] * n_vmem,
        out_specs=specs if many else specs[0],
        scratch_shapes=list(scratch),
        compiler_params=pltpu.CompilerParams(vmem_limit_bytes=40 * 2**20),
        name=name,
    )


def shards(child_front, parent_front, block_map):
    leaf_id = lax.axis_index("leaf")
    row_id = lax.axis_index("row")
    col_id = lax.axis_index("col")
    row_count = lax.axis_size("row")
    col_count = lax.axis_size("col")
    leaf_count = lax.axis_size("leaf")
    half_id = leaf_id % 2
    ids = jnp.stack([half_id, row_id, col_id]).astype(jnp.int32)
    own_map = lax.dynamic_index_in_dim(block_map, leaf_id, 0, keepdims=False)
    partner_map = lax.dynamic_index_in_dim(block_map, leaf_id ^ 1, 0, keepdims=False)
    count = own_map.shape[0]

    child_block = child_front[0]
    child_rows, child_cols = child_block.shape
    width = child_cols // 2
    parent_rows, parent_cols = parent_front.shape
    row_span, col_span = parent_rows // BLK, parent_cols // BLK
    row_blocks, col_blocks = child_rows // BLK, child_cols // BLK
    first = width // BLK
    cap = -(-count // row_count)
    swap = [(i, i ^ 1) for i in range(leaf_count)]

    def only(cell, got, value, targets):
        index = lax.axis_index(cell)
        hit = functools.reduce(jnp.logical_or, [index == t for t in targets])
        return jnp.where(hit, got, value)

    strips = kernel_call(
        functools.partial(strips_kernel, (row_span, first, row_blocks)),
        "strips", (row_count, BLK, child_cols), 2, 1,
    )(ids, own_map, child_block)
    strips, child_block = lax.optimization_barrier((strips, child_block))
    got = lax.all_to_all(strips, "row", 0, 0, tiled=True)

    def by_rows(pairs):
        return [(r * col_count, q * col_count) for r, q in pairs]

    diagonal, slab, top = child_block[:width, :width], child_block[:, :width], child_block[:width]
    for pairs in HALVING:
        targets = [t for _, t in pairs]
        diagonal = only("row", send(diagonal, ("row", "col"), by_rows(pairs)), diagonal, targets)
        slab = only("col", send(slab, "col", pairs), slab, targets)
        top = only("row", send(top, "row", pairs), top, targets)
        diagonal, slab, top = lax.optimization_barrier((diagonal, slab, top))
    for pairs in HALVING:
        diagonal = only("col", send(diagonal, "col", pairs), diagonal, [t for _, t in pairs])
    inverse = inverse_factor(diagonal)
    cols_factor = jnp.dot(inverse, top, precision=HIGHEST)
    out_width = width // col_count
    share = lax.dynamic_slice_in_dim(inverse, col_id * out_width, out_width, 0)
    child_out = lax.dot_general(share, slab, (((1,), (1,)), ((), ())), precision=HIGHEST)
    piece = (out_width, BLK)
    row_slots = kernel_call(
        functools.partial(row_slots_kernel, (row_span, first, row_blocks)),
        "row_slots", (row_count,) + piece, 2, 1,
    )(ids, own_map, child_out)
    col_share = lax.dynamic_slice_in_dim(cols_factor, row_id * out_width, out_width, 0)
    col_slots = kernel_call(
        functools.partial(col_slots_kernel, (col_span, first, col_blocks, col_count)),
        "col_slots", (col_count,) + piece, 2, 1,
    )(ids, own_map, col_share)
    got, row_slots, col_slots = lax.optimization_barrier((got, row_slots, col_slots))
    tables = [pltpu.SMEM((count,), jnp.int32), pltpu.SMEM((cap,), jnp.int32)]
    tiles = kernel_call(
        functools.partial(
            tiles_kernel,
            (row_span, col_span, first, row_blocks, col_blocks, col_count, count),
        ),
        "tiles", (col_count, cap, BLK, BLK), 2, 1, tables,
    )(ids, own_map, got)
    tiles, row_slots, col_slots = lax.optimization_barrier((tiles, row_slots, col_slots))
    landed = lax.all_to_all(
        tiles.reshape(col_count, cap * BLK, BLK), "col", 0, 0, tiled=True
    ).reshape(tiles.shape)

    row_got = lax.all_to_all(row_slots, "row", 0, 0, tiled=True)
    col_slots, row_got = lax.optimization_barrier((col_slots, row_got))
    col_got = lax.all_to_all(col_slots, "col", 0, 0, tiled=True)
    row_panel = kernel_call(
        functools.partial(row_pick_kernel, (row_span, first, row_blocks, count)),
        "row_pick", (cap,) + piece, 2, 1, tables,
    )(ids, own_map, row_got)
    own_cols, other_cols = kernel_call(
        functools.partial(col_pick_kernel, (col_span, first, col_blocks, col_count, count)),
        "col_pick", [(col_span,) + piece] * 2, 2, 1,
    )(ids, own_map, col_got)

    def doubled(value, axis, bit):
        got = send(value, axis, [(i, i ^ (1 << bit)) for i in range(lax.axis_size(axis))])
        upper = (lax.axis_index(axis) >> bit) & 1
        low = jnp.where(upper == 0, value, got)
        high = jnp.where(upper == 0, got, value)
        return jnp.stack([low, high])

    row_panel = doubled(row_panel, "col", 2)
    col_panels = jnp.stack([own_cols, send(other_cols, "leaf", swap)])
    row_panel, col_panels = lax.optimization_barrier((row_panel, col_panels))
    row_panel = doubled(row_panel, "col", 1)
    col_panels = doubled(col_panels, "row", 0)
    row_panel, col_panels = lax.optimization_barrier((row_panel, col_panels))
    row_panel = doubled(row_panel, "col", 0)
    col_panels = doubled(col_panels, "row", 1)
    row_panel, col_panels = lax.optimization_barrier((row_panel, col_panels))
    row_panel = jnp.transpose(row_panel, (2, 1, 0, 4, 3, 5)).reshape(width, cap * BLK)
    pair_row_panel = send(row_panel, "leaf", swap)
    col_panels = doubled(col_panels, "row", 2)
    col_panels = jnp.transpose(col_panels, (3, 0, 1, 2, 5, 4, 6))
    col_panels = col_panels.reshape(2, width, col_span * BLK)

    def product(rows, cols):
        return lax.dot_general(rows, cols, (((0,), (0,)), ((), ())), precision=HIGHEST)

    own_product = product(row_panel, col_panels[0])
    pair_product = product(pair_row_panel, col_panels[1])
    landed, own_product, pair_product = lax.optimization_barrier(
        (landed, own_product, pair_product)
    )
    other = kernel_call(
        functools.partial(other_kernel, (col_span, first, col_blocks, col_count, count)),
        "other", (col_span, cap, BLK, BLK), 2, 1,
    )(ids, own_map, landed)
    other = send(other, "leaf", swap)
    assembled = kernel_call(
        functools.partial(
            assemble_kernel, (row_span, col_span, first, col_blocks, col_count, count)
        ),
        "assemble", parent_front.shape, 3, 5,
        tables + [pltpu.SMEM((cap,), jnp.int32)],
    )(ids, own_map, partner_map, parent_front, own_product, pair_product, other, landed)

    parent_order = parent_rows * row_count
    parent_width = parent_cols // 2
    even = range(0, leaf_count, 2)
    grid = row_count * col_count
    across = [(l, l + 1) for l in even]
    diagonal = assembled[:parent_width, :parent_width]
    slab, top = assembled[:, :parent_width], assembled[:parent_width]
    diagonal, slab, top = lax.optimization_barrier((diagonal, slab, top))

    def spread_rows(value, pairs):
        moves = [
            (l * grid + r * col_count, l * grid + q * col_count) for l in even for r, q in pairs
        ]
        return send(value, ("leaf", "row", "col"), moves)

    def spread_cols(value, pairs):
        moves = [(l * col_count + r, l * col_count + q) for l in even for r, q in pairs]
        return only("col", send(value, ("leaf", "col"), moves), value, [q for _, q in pairs])

    def spread_top(value, pairs):
        return only("row", send(value, "row", pairs), value, [q for _, q in pairs])

    fan = [spread_rows(diagonal, [(0, q)]) for q in (2, 4, 6)]
    diagonal = only("row", functools.reduce(jnp.add, fan), diagonal, (2, 4, 6))
    slab = spread_cols(slab, HALVING[0])
    (diagonal,) = lax.optimization_barrier([diagonal])
    zhi = [(0, 1), (2, 3), (4, 5), (6, 7)]
    diagonal = only("row", spread_rows(diagonal, zhi), diagonal, (1, 3, 5, 7))
    top = spread_top(top, HALVING[0])
    diagonal, slab, top = lax.optimization_barrier((diagonal, slab, top))
    diagonal = spread_cols(diagonal, HALVING[0])
    slab = spread_cols(slab, HALVING[1])
    top = spread_top(top, HALVING[1])
    diagonal, slab, top = lax.optimization_barrier((diagonal, slab, top))
    diagonal = spread_cols(diagonal, HALVING[1])
    slab = spread_cols(slab, HALVING[2])
    top = spread_top(top, HALVING[2])
    diagonal, slab = lax.optimization_barrier((diagonal, slab))
    diagonal = spread_cols(diagonal, HALVING[2])
    diagonal = jnp.where(half_id == 0, diagonal, send(diagonal, "leaf", across))
    slab = jnp.where(half_id == 0, slab, send(slab, "leaf", across))
    inverse = inverse_factor(diagonal)
    rows_factor = lax.dot_general(slab, inverse, (((1,), (1,)), ((), ())), precision=HIGHEST)
    cols_factor = jnp.dot(inverse, top, precision=HIGHEST)
    update = jnp.dot(rows_factor, cols_factor, precision=HIGHEST)
    row_ids = row_id * parent_rows + jnp.arange(parent_rows)
    col_ids = half_id * (parent_order // 2) + col_id * parent_cols + jnp.arange(parent_cols)
    keep = (row_ids[:, None] >= parent_width) & (col_ids[None, :] >= parent_width)
    parent_schur = jnp.where(keep, assembled - update, jnp.float32(0.0))
    share = parent_width // (2 * col_count)
    start = (half_id * col_count + col_id) * share
    parent_out = lax.dynamic_slice_in_dim(rows_factor, start, share, 1).T
    return (child_out[None], parent_out, parent_schur)


def solution(mesh):
    placed = (P("leaf", "row", "col"), P("row", ("leaf", "col")), P())
    return jax.shard_map(
        shards,
        mesh=mesh,
        in_specs=placed,
        out_specs=(P("leaf", "col", "row"), P(("leaf", "col"), "row"), P("row", ("leaf", "col"))),
        check_vma=False,
    )
```

```python
import functools

import jax
import jax.numpy as jnp
from jax import lax
from jax.experimental import pallas as pl
from jax.experimental.pallas import tpu as pltpu
from jax.sharding import PartitionSpec as P

BLK = 128
STEP = 64
GROUP = 8
HIGHEST = lax.Precision.HIGHEST


def send(value, axes, pairs):
    return lax.ppermute(value, axes, pairs)


HALVING = ([(0, 4)], [(0, 2), (4, 6)], [(0, 1), (2, 3), (4, 5), (6, 7)])


def reciprocal(x):
    guess = pltpu.reciprocal(x, approx=True)
    guess = guess * (2.0 - x * guess)
    return guess * (2.0 - x * guess)


def inverse_factor_kernel(a_ref, out_ref, x_ref):
    order = a_ref.shape[0]
    f32 = jnp.float32
    value = a_ref[...]
    full_sub = lax.broadcasted_iota(jnp.int32, value.shape, 0)
    full_lane = lax.broadcasted_iota(jnp.int32, value.shape, 1)
    diagonal = jnp.where(full_sub == full_lane, value, 0.0)
    scale_col = lax.rsqrt(jnp.sum(diagonal, axis=1, keepdims=True))
    scale_row = lax.rsqrt(jnp.sum(diagonal, axis=0, keepdims=True))
    x_ref[...] = (value * scale_col) * scale_row
    wide = (STEP, 2 * STEP)
    sub = lax.broadcasted_iota(jnp.int32, wide, 0)
    lane = lax.broadcasted_iota(jnp.int32, wide, 1)
    eye = (sub[:, :STEP] == lane[:, :STEP]).astype(f32)
    for start in range(0, order, STEP):
        stop = start + STEP
        rows = x_ref[start:stop, :]
        work = jnp.concatenate([x_ref[start:stop, start:stop], eye], axis=1)
        for base in range(0, STEP, GROUP):
            cols = [
                jnp.broadcast_to(work[:, base + j : base + j + 1], wide) for j in range(GROUP)
            ]
            for j in range(0, GROUP, 2):
                k = base + j
                c0, c1 = cols[j], cols[j + 1]
                p00, p01, p11 = c0[k : k + 1], c1[k : k + 1], c1[k + 1 : k + 2]
                over = reciprocal(p00 * p11 - p01 * p01)
                a00, a01, a11 = p00 * over, p01 * over, p11 * over
                below = sub > k + 1
                f0 = jnp.where(below, c0 * a11 - c1 * a01, 0.0)
                f1 = jnp.where(below, c1 * a00 - c0 * a01, 0.0)
                for i in range(j + 2, GROUP):
                    cols[i] = cols[i] - f0 * cols[i][k : k + 1] - f1 * cols[i][k + 1 : k + 2]
                work = work - f0 * work[k : k + 1] - f1 * work[k + 1 : k + 2]
        pivots = jnp.sum(jnp.where(sub == lane, work, 0.0), axis=1, keepdims=True)
        left = jnp.sum(jnp.where(sub == lane + 1, work, 0.0), axis=1, keepdims=True)
        above = pltpu.roll(jnp.broadcast_to(pivots, wide), 1, 0)
        work = work - jnp.where(sub % 2 == 1, left / above, 0.0) * pltpu.roll(work, 1, 0)
        pivots = jnp.sum(jnp.where(sub == lane, work, 0.0), axis=1, keepdims=True)
        inverse = work[:, STEP:] * lax.rsqrt(pivots)
        panel = jnp.dot(inverse, rows, precision=HIGHEST, preferred_element_type=f32)
        pieces = [inverse]
        if start:
            pieces.insert(0, panel[:, :start])
        if stop < order:
            pieces.append(panel[:, stop:])
        panel = jnp.concatenate(pieces, axis=1)
        x_ref[start:stop, :] = panel
        if stop < order:
            change = lax.dot_general(
                panel[:, stop:], panel, (((0,), (0,)), ((), ())),
                precision=HIGHEST, preferred_element_type=f32,
            )
            old = x_ref[stop:, :]
            at = lax.broadcasted_iota(jnp.int32, old.shape, 1)
            x_ref[stop:, :] = jnp.where((at >= start) & (at < stop), 0.0, old) - change
    out_ref[...] = jnp.where(full_lane <= full_sub, x_ref[...] * scale_row, 0.0)


def inverse_factor(block):
    return pl.pallas_call(
        inverse_factor_kernel,
        out_shape=jax.ShapeDtypeStruct(block.shape, jnp.float32),
        scratch_shapes=[pltpu.VMEM(block.shape, jnp.float32)],
        name="inverse_factor",
    )(block)


def smem():
    return pl.BlockSpec(memory_space=pltpu.SMEM)


def vmem():
    return pl.BlockSpec(memory_space=pltpu.VMEM)


def row_tables(map_ref, row, row_span, count, rank_ref, at_ref):
    for m in range(at_ref.shape[0]):
        at_ref[m] = -1

    def body(k, rank):
        here = map_ref[k] // row_span == row
        rank_ref[k] = jnp.where(here, rank, -1)

        @pl.when(here)
        def _():
            at_ref[jnp.minimum(rank, at_ref.shape[0] - 1)] = map_ref[k] % row_span

        return rank + here.astype(jnp.int32)

    lax.fori_loop(0, count, body, jnp.int32(0))


def strips_kernel(sizes, ids_ref, map_ref, part_ref, out_ref):
    row_span, first, row_blocks = sizes
    row = ids_ref[1]
    for a in range(row_blocks):
        block = row * row_blocks + a - first

        @pl.when(block >= 0)
        def _():
            target = map_ref[jnp.maximum(block, 0)] // row_span
            out_ref[target] = part_ref[a * BLK : (a + 1) * BLK, :]


def tiles_kernel(sizes, ids_ref, map_ref, got_ref, out_ref, rank_ref, at_ref):
    row_span, col_span, first, row_blocks, col_blocks, cols, count = sizes
    row, col = ids_ref[1], ids_ref[2]
    row_tables(map_ref, row, row_span, count, rank_ref, at_ref)

    def body(k, carry):
        rank = rank_ref[k]

        @pl.when(rank >= 0)
        def _():
            source = (k + first) // row_blocks
            slot = jnp.minimum(rank, out_ref.shape[1] - 1)
            for y in range(col_blocks):
                block = col * col_blocks + y - first

                @pl.when(block >= 0)
                def _():
                    target = (map_ref[jnp.maximum(block, 0)] // col_span) % cols
                    out_ref[target, slot] = got_ref[source, :, y * BLK : (y + 1) * BLK]

        return carry

    lax.fori_loop(0, count, body, jnp.int32(0))


def other_kernel(sizes, ids_ref, map_ref, landed_ref, out_ref):
    col_span, first, col_blocks, cols, count = sizes
    half, col = ids_ref[0], ids_ref[2]
    out_ref[...] = jnp.zeros_like(out_ref)

    def body(k, carry):
        owner = map_ref[k] // col_span

        @pl.when((owner % cols == col) & (owner // cols != half))
        def _():
            out_ref[map_ref[k] % col_span] = landed_ref[(k + first) // col_blocks]

        return carry

    lax.fori_loop(0, count, body, jnp.int32(0))


def assemble_kernel(sizes, ids_ref, map_ref, pair_map_ref, parent_ref, other_ref, landed_ref,
                    out_ref, diagonal_ref, slab_ref, top_ref, rank_ref, at_ref, pair_at_ref):
    row_span, col_span, first, col_blocks, cols, count = sizes
    half, row, col = ids_ref[0], ids_ref[1], ids_ref[2]
    out_ref[...] = parent_ref[...].astype(jnp.float32)
    row_tables(pair_map_ref, row, row_span, count, rank_ref, pair_at_ref)
    row_tables(map_ref, row, row_span, count, rank_ref, at_ref)
    caps = at_ref.shape[0]
    for m in range(caps):
        at = pair_at_ref[m]

        @pl.when(at >= 0)
        def _():
            for y in range(col_span):
                spot = (
                    pl.ds(pl.multiple_of(at * BLK, BLK), BLK), slice(y * BLK, (y + 1) * BLK)
                )
                out_ref[spot] = out_ref[spot] + other_ref[y, m]

    def body(k, carry):
        owner = map_ref[k] // col_span

        @pl.when((owner % cols == col) & (owner // cols == half))
        def _():
            at_col = pl.ds(pl.multiple_of((map_ref[k] % col_span) * BLK, BLK), BLK)
            for m in range(caps):
                at = at_ref[m]

                @pl.when(at >= 0)
                def _():
                    spot = (pl.ds(pl.multiple_of(at * BLK, BLK), BLK), at_col)
                    out_ref[spot] = out_ref[spot] + landed_ref[(k + first) // col_blocks, m]

        return carry

    lax.fori_loop(0, count, body, jnp.int32(0))
    width = diagonal_ref.shape[0]
    diagonal_ref[...] = out_ref[:width, :width]
    slab_ref[...] = out_ref[:, :width]
    top_ref[...] = out_ref[:width, :]


def kernel_call(body, name, outs, n_smem, n_vmem, scratch=()):
    many = isinstance(outs, list)
    shapes = [jax.ShapeDtypeStruct(o, jnp.float32) for o in (outs if many else [outs])]
    specs = [vmem() for _ in shapes]
    return pl.pallas_call(
        body,
        out_shape=shapes if many else shapes[0],
        in_specs=[smem()] * n_smem + [vmem()] * n_vmem,
        out_specs=specs if many else specs[0],
        scratch_shapes=list(scratch),
        compiler_params=pltpu.CompilerParams(vmem_limit_bytes=40 * 2**20),
        name=name,
    )


def shards(child_front, parent_front, block_map):
    leaf_id = lax.axis_index("leaf")
    row_id = lax.axis_index("row")
    col_id = lax.axis_index("col")
    row_count = lax.axis_size("row")
    col_count = lax.axis_size("col")
    leaf_count = lax.axis_size("leaf")
    half_id = leaf_id % 2
    ids = jnp.stack([half_id, row_id, col_id]).astype(jnp.int32)
    own_map = lax.dynamic_index_in_dim(block_map, leaf_id, 0, keepdims=False)
    partner_map = lax.dynamic_index_in_dim(block_map, leaf_id ^ 1, 0, keepdims=False)
    count = own_map.shape[0]

    child_block = child_front[0]
    child_rows, child_cols = child_block.shape
    width = child_cols // 2
    parent_rows, parent_cols = parent_front.shape
    row_span, col_span = parent_rows // BLK, parent_cols // BLK
    row_blocks, col_blocks = child_rows // BLK, child_cols // BLK
    first = width // BLK
    cap = -(-count // row_count)
    swap = [(i, i ^ 1) for i in range(leaf_count)]

    def only(axis, got, value, targets):
        index = lax.axis_index(axis)
        hit = functools.reduce(jnp.logical_or, [index == t for t in targets])
        return jnp.where(hit, got, value)

    def after(value, earlier):
        return lax.optimization_barrier((value, earlier))[0]

    grid = row_count * col_count
    zhi = [(r, r + 1) for r in range(0, row_count, 2)]
    fan = list(range(2, row_count, 2))

    def panel_parts(diagonal, slab, top, leaves, paired):
        def down(value, pairs):
            moves = [
                (l * grid + r * col_count, l * grid + q * col_count)
                for l in leaves for r, q in pairs
            ]
            return send(value, ("leaf", "row", "col"), moves)

        def along(value, pairs):
            moves = [(l * col_count + r, l * col_count + q) for l in leaves for r, q in pairs]
            got = send(value, ("leaf", "col"), moves)
            return only("col", got, value, [q for _, q in pairs])

        def over(value, pairs):
            return only("row", send(value, "row", pairs), value, [q for _, q in pairs])

        first_hop = functools.reduce(jnp.add, [down(diagonal, [(0, q)]) for q in fan])
        d1 = only("row", first_hop, diagonal, fan)
        slab1 = along(slab, HALVING[0])
        top1 = over(top, HALVING[0])
        d2 = only("row", down(d1, zhi), d1, [q for _, q in zhi])
        d3 = along(d2, HALVING[0])
        slab2 = along(after(slab1, d2), HALVING[1])
        top2 = over(after(top1, d2), HALVING[1])
        d4 = along(d3, HALVING[1])
        slab3 = along(after(slab2, d3), HALVING[2])
        top3 = over(after(top2, d3), HALVING[2])
        d5 = along(d4, HALVING[2])
        if paired:
            across = [(l, l + 1) for l in leaves]
            d5 = jnp.where(half_id == 0, d5, send(d5, "leaf", across))
            slab3 = jnp.where(half_id == 0, slab3, send(slab3, "leaf", across))
        return d5, slab3, top3

    diagonal, slab, top = panel_parts(
        child_block[:width, :width], child_block[:, :width], child_block[:width],
        list(range(leaf_count)), False,
    )
    inverse = inverse_factor(diagonal)
    rows_factor = lax.dot_general(slab, inverse, (((1,), (1,)), ((), ())), precision=HIGHEST)
    cols_factor = jnp.dot(inverse, top, precision=HIGHEST)
    contribution = child_block - jnp.dot(rows_factor, cols_factor, precision=HIGHEST)
    out_width = width // col_count
    child_out = lax.dynamic_slice_in_dim(rows_factor, col_id * out_width, out_width, 1).T

    strips = kernel_call(
        functools.partial(strips_kernel, (row_span, first, row_blocks)),
        "strips", (row_count, BLK, child_cols), 2, 1,
    )(ids, own_map, contribution)
    got = lax.all_to_all(strips, "row", 0, 0, tiled=True)
    tables = [pltpu.SMEM((count,), jnp.int32), pltpu.SMEM((cap,), jnp.int32)]
    tiles = kernel_call(
        functools.partial(
            tiles_kernel,
            (row_span, col_span, first, row_blocks, col_blocks, col_count, count),
        ),
        "tiles", (col_count, cap, BLK, BLK), 2, 1, tables,
    )(ids, own_map, got)
    landed = lax.all_to_all(
        tiles.reshape(col_count, cap * BLK, BLK), "col", 0, 0, tiled=True
    ).reshape(tiles.shape)
    other = kernel_call(
        functools.partial(other_kernel, (col_span, first, col_blocks, col_count, count)),
        "other", (col_span, cap, BLK, BLK), 2, 1,
    )(ids, own_map, landed)
    other = send(other, "leaf", swap)

    parent_order = parent_rows * row_count
    parent_width = parent_cols // 2
    assembled, diagonal, slab, top = kernel_call(
        functools.partial(
            assemble_kernel, (row_span, col_span, first, col_blocks, col_count, count)
        ),
        "assemble",
        [
            parent_front.shape, (parent_width, parent_width),
            (parent_rows, parent_width), (parent_width, parent_cols),
        ],
        3, 3, tables + [pltpu.SMEM((cap,), jnp.int32)],
    )(ids, own_map, partner_map, parent_front, other, landed)
    diagonal, slab, top = panel_parts(
        diagonal, slab, top, list(range(0, leaf_count, 2)), True
    )
    inverse = inverse_factor(diagonal)
    rows_factor = lax.dot_general(slab, inverse, (((1,), (1,)), ((), ())), precision=HIGHEST)
    cols_factor = jnp.dot(inverse, top, precision=HIGHEST)
    update = jnp.dot(rows_factor, cols_factor, precision=HIGHEST)
    row_ids = row_id * parent_rows + jnp.arange(parent_rows)
    col_ids = half_id * (parent_order // 2) + col_id * parent_cols + jnp.arange(parent_cols)
    keep = (row_ids[:, None] >= parent_width) & (col_ids[None, :] >= parent_width)
    parent_schur = jnp.where(keep, assembled - update, jnp.float32(0.0))
    share = parent_width // (2 * col_count)
    start = (half_id * col_count + col_id) * share
    parent_out = lax.dynamic_slice_in_dim(rows_factor, start, share, 1).T
    return (child_out[None], parent_out, parent_schur)


def solution(mesh):
    placed = (P("leaf", "row", "col"), P("row", ("leaf", "col")), P())
    return jax.shard_map(
        shards,
        mesh=mesh,
        in_specs=placed,
        out_specs=(P("leaf", "col", "row"), P(("leaf", "col"), "row"), P("row", ("leaf", "col"))),
        check_vma=False,
    )
```

```python
import functools

import jax
import jax.numpy as jnp
from jax import lax
from jax.experimental import pallas as pl
from jax.experimental.pallas import tpu as pltpu
from jax.sharding import PartitionSpec as P

BLK = 128
STEP = 64
GROUP = 8
HIGHEST = lax.Precision.HIGHEST


def send(value, axes, pairs):
    return lax.ppermute(value, axes, pairs)


HALVING = ([(0, 4)], [(0, 2), (4, 6)], [(0, 1), (2, 3), (4, 5), (6, 7)])


def reciprocal(x):
    guess = pltpu.reciprocal(x, approx=True)
    guess = guess * (2.0 - x * guess)
    return guess * (2.0 - x * guess)


def inverse_factor_kernel(a_ref, out_ref, x_ref):
    order = a_ref.shape[0]
    f32 = jnp.float32
    value = a_ref[...]
    full_sub = lax.broadcasted_iota(jnp.int32, value.shape, 0)
    full_lane = lax.broadcasted_iota(jnp.int32, value.shape, 1)
    diagonal = jnp.where(full_sub == full_lane, value, 0.0)
    scale_col = lax.rsqrt(jnp.sum(diagonal, axis=1, keepdims=True))
    scale_row = lax.rsqrt(jnp.sum(diagonal, axis=0, keepdims=True))
    x_ref[...] = (value * scale_col) * scale_row
    wide = (STEP, 2 * STEP)
    sub = lax.broadcasted_iota(jnp.int32, wide, 0)
    lane = lax.broadcasted_iota(jnp.int32, wide, 1)
    eye = (sub[:, :STEP] == lane[:, :STEP]).astype(f32)
    for start in range(0, order, STEP):
        stop = start + STEP
        rows = x_ref[start:stop, :]
        work = jnp.concatenate([x_ref[start:stop, start:stop], eye], axis=1)
        for base in range(0, STEP, GROUP):
            cols = [
                jnp.broadcast_to(work[:, base + j : base + j + 1], wide) for j in range(GROUP)
            ]
            for j in range(0, GROUP, 2):
                k = base + j
                c0, c1 = cols[j], cols[j + 1]
                p00, p01, p11 = c0[k : k + 1], c1[k : k + 1], c1[k + 1 : k + 2]
                over = reciprocal(p00 * p11 - p01 * p01)
                a00, a01, a11 = p00 * over, p01 * over, p11 * over
                below = sub > k + 1
                f0 = jnp.where(below, c0 * a11 - c1 * a01, 0.0)
                f1 = jnp.where(below, c1 * a00 - c0 * a01, 0.0)
                for i in range(j + 2, GROUP):
                    cols[i] = cols[i] - f0 * cols[i][k : k + 1] - f1 * cols[i][k + 1 : k + 2]
                work = work - f0 * work[k : k + 1] - f1 * work[k + 1 : k + 2]
        pivots = jnp.sum(jnp.where(sub == lane, work, 0.0), axis=1, keepdims=True)
        left = jnp.sum(jnp.where(sub == lane + 1, work, 0.0), axis=1, keepdims=True)
        above = pltpu.roll(jnp.broadcast_to(pivots, wide), 1, 0)
        work = work - jnp.where(sub % 2 == 1, left / above, 0.0) * pltpu.roll(work, 1, 0)
        pivots = jnp.sum(jnp.where(sub == lane, work, 0.0), axis=1, keepdims=True)
        inverse = work[:, STEP:] * lax.rsqrt(pivots)
        panel = jnp.dot(inverse, rows, precision=HIGHEST, preferred_element_type=f32)
        pieces = [inverse]
        if start:
            pieces.insert(0, panel[:, :start])
        if stop < order:
            pieces.append(panel[:, stop:])
        panel = jnp.concatenate(pieces, axis=1)
        x_ref[start:stop, :] = panel
        if stop < order:
            change = lax.dot_general(
                panel[:, stop:], panel, (((0,), (0,)), ((), ())),
                precision=HIGHEST, preferred_element_type=f32,
            )
            old = x_ref[stop:, :]
            at = lax.broadcasted_iota(jnp.int32, old.shape, 1)
            x_ref[stop:, :] = jnp.where((at >= start) & (at < stop), 0.0, old) - change
    out_ref[...] = jnp.where(full_lane <= full_sub, x_ref[...] * scale_row, 0.0)


def inverse_factor(block):
    return pl.pallas_call(
        inverse_factor_kernel,
        out_shape=jax.ShapeDtypeStruct(block.shape, jnp.float32),
        scratch_shapes=[pltpu.VMEM(block.shape, jnp.float32)],
        name="inverse_factor",
    )(block)


def smem():
    return pl.BlockSpec(memory_space=pltpu.SMEM)


def vmem():
    return pl.BlockSpec(memory_space=pltpu.VMEM)


def row_tables(map_ref, row, row_span, count, rank_ref, at_ref):
    for m in range(at_ref.shape[0]):
        at_ref[m] = -1

    def body(k, rank):
        here = map_ref[k] // row_span == row
        rank_ref[k] = jnp.where(here, rank, -1)

        @pl.when(here)
        def _():
            at_ref[jnp.minimum(rank, at_ref.shape[0] - 1)] = map_ref[k] % row_span

        return rank + here.astype(jnp.int32)

    lax.fori_loop(0, count, body, jnp.int32(0))


def strips_kernel(sizes, ids_ref, map_ref, part_ref, out_ref):
    row_span, first, row_blocks = sizes
    row = ids_ref[1]
    for a in range(row_blocks):
        block = row * row_blocks + a - first

        @pl.when(block >= 0)
        def _():
            target = map_ref[jnp.maximum(block, 0)] // row_span
            out_ref[target] = part_ref[a * BLK : (a + 1) * BLK, :]


def tiles_kernel(sizes, ids_ref, map_ref, got_ref, out_ref, rank_ref, at_ref):
    row_span, col_span, first, row_blocks, col_blocks, cols, count = sizes
    row, col = ids_ref[1], ids_ref[2]
    row_tables(map_ref, row, row_span, count, rank_ref, at_ref)

    def body(k, carry):
        rank = rank_ref[k]

        @pl.when(rank >= 0)
        def _():
            source = (k + first) // row_blocks
            slot = jnp.minimum(rank, out_ref.shape[1] - 1)
            for y in range(col_blocks):
                block = col * col_blocks + y - first

                @pl.when(block >= 0)
                def _():
                    target = (map_ref[jnp.maximum(block, 0)] // col_span) % cols
                    out_ref[target, slot] = got_ref[source, :, y * BLK : (y + 1) * BLK]

        return carry

    lax.fori_loop(0, count, body, jnp.int32(0))


def other_kernel(sizes, ids_ref, map_ref, landed_ref, out_ref):
    col_span, first, col_blocks, cols, count = sizes
    half, col = ids_ref[0], ids_ref[2]
    out_ref[...] = jnp.zeros_like(out_ref)

    def body(k, carry):
        owner = map_ref[k] // col_span

        @pl.when((owner % cols == col) & (owner // cols != half))
        def _():
            out_ref[map_ref[k] % col_span] = landed_ref[(k + first) // col_blocks]

        return carry

    lax.fori_loop(0, count, body, jnp.int32(0))


def assemble_kernel(sizes, ids_ref, map_ref, pair_map_ref, parent_ref, other_ref, landed_ref,
                    out_ref, diagonal_ref, slab_ref, top_ref, rank_ref, at_ref, pair_at_ref):
    row_span, col_span, first, col_blocks, cols, count = sizes
    half, row, col = ids_ref[0], ids_ref[1], ids_ref[2]
    out_ref[...] = parent_ref[...].astype(jnp.float32)
    row_tables(pair_map_ref, row, row_span, count, rank_ref, pair_at_ref)
    row_tables(map_ref, row, row_span, count, rank_ref, at_ref)
    caps = at_ref.shape[0]
    for m in range(caps):
        at = pair_at_ref[m]

        @pl.when(at >= 0)
        def _():
            for y in range(col_span):
                spot = (
                    pl.ds(pl.multiple_of(at * BLK, BLK), BLK), slice(y * BLK, (y + 1) * BLK)
                )
                out_ref[spot] = out_ref[spot] + other_ref[y, m]

    def body(k, carry):
        owner = map_ref[k] // col_span

        @pl.when((owner % cols == col) & (owner // cols == half))
        def _():
            at_col = pl.ds(pl.multiple_of((map_ref[k] % col_span) * BLK, BLK), BLK)
            for m in range(caps):
                at = at_ref[m]

                @pl.when(at >= 0)
                def _():
                    spot = (pl.ds(pl.multiple_of(at * BLK, BLK), BLK), at_col)
                    out_ref[spot] = out_ref[spot] + landed_ref[(k + first) // col_blocks, m]

        return carry

    lax.fori_loop(0, count, body, jnp.int32(0))
    width = diagonal_ref.shape[0]
    diagonal_ref[...] = out_ref[:width, :width]
    slab_ref[...] = out_ref[:, :width]
    top_ref[...] = out_ref[:width, :]


def kernel_call(body, name, outs, n_smem, n_vmem, scratch=()):
    many = isinstance(outs, list)
    shapes = [jax.ShapeDtypeStruct(o, jnp.float32) for o in (outs if many else [outs])]
    specs = [vmem() for _ in shapes]
    return pl.pallas_call(
        body,
        out_shape=shapes if many else shapes[0],
        in_specs=[smem()] * n_smem + [vmem()] * n_vmem,
        out_specs=specs if many else specs[0],
        scratch_shapes=list(scratch),
        compiler_params=pltpu.CompilerParams(vmem_limit_bytes=40 * 2**20),
        name=name,
    )


def shards(child_front, parent_front, block_map):
    leaf_id = lax.axis_index("leaf")
    row_id = lax.axis_index("row")
    col_id = lax.axis_index("col")
    row_count = lax.axis_size("row")
    col_count = lax.axis_size("col")
    leaf_count = lax.axis_size("leaf")
    half_id = leaf_id % 2
    ids = jnp.stack([half_id, row_id, col_id]).astype(jnp.int32)
    own_map = lax.dynamic_index_in_dim(block_map, leaf_id, 0, keepdims=False)
    partner_map = lax.dynamic_index_in_dim(block_map, leaf_id ^ 1, 0, keepdims=False)
    count = own_map.shape[0]

    child_block = child_front[0]
    child_rows, child_cols = child_block.shape
    width = child_cols // 2
    parent_rows, parent_cols = parent_front.shape
    row_span, col_span = parent_rows // BLK, parent_cols // BLK
    row_blocks, col_blocks = child_rows // BLK, child_cols // BLK
    first = width // BLK
    cap = -(-count // row_count)
    swap = [(i, i ^ 1) for i in range(leaf_count)]

    def only(axis, got, value, targets):
        index = lax.axis_index(axis)
        hit = functools.reduce(jnp.logical_or, [index == t for t in targets])
        return jnp.where(hit, got, value)

    def after(value, earlier):
        return lax.optimization_barrier((value, earlier))[0]

    grid = row_count * col_count
    fan = list(range(2, row_count, 2))

    def panel_parts(diagonal, slab, top, leaves, paired):
        def down(value, pairs):
            moves = [
                (l * grid + r * col_count, l * grid + q * col_count)
                for l in leaves for r, q in pairs
            ]
            return send(value, ("leaf", "row", "col"), moves)

        def along(value, pairs):
            moves = [(l * col_count + r, l * col_count + q) for l in leaves for r, q in pairs]
            got = send(value, ("leaf", "col"), moves)
            return only("col", got, value, [q for _, q in pairs])

        def over(value, pairs):
            return only("row", send(value, "row", pairs), value, [q for _, q in pairs])

        d1 = only("row", down(diagonal, [(0, 1)]), diagonal, [1])
        slab1 = along(slab, HALVING[0])
        top1 = over(top, [(0, 1)])
        hops = [[(0, q), (1, q + 1)] for q in fan]
        d2 = functools.reduce(jnp.add, [down(d1, pairs) for pairs in hops])
        d2 = only("row", d2, d1, [q for pairs in hops for _, q in pairs])
        d3 = along(d2, HALVING[0])
        slab2 = along(after(slab1, d2), HALVING[1])
        top2 = over(after(top1, d2), [(0, 4), (1, 5)])
        d4 = along(d3, HALVING[1])
        slab3 = along(after(slab2, d3), HALVING[2])
        top3 = over(after(top2, d3), [(0, 2), (1, 3), (4, 6), (5, 7)])
        d5 = along(d4, HALVING[2])
        if paired:
            across = [(l, l + 1) for l in leaves]
            d5 = jnp.where(half_id == 0, d5, send(d5, "leaf", across))
            slab3 = jnp.where(half_id == 0, slab3, send(slab3, "leaf", across))
        return d5, slab3, top3

    diagonal, slab, top = panel_parts(
        child_block[:width, :width], child_block[:, :width], child_block[:width],
        list(range(leaf_count)), False,
    )
    inverse = inverse_factor(diagonal)
    rows_factor = lax.dot_general(slab, inverse, (((1,), (1,)), ((), ())), precision=HIGHEST)
    cols_factor = jnp.dot(inverse, top, precision=HIGHEST)
    contribution = child_block - jnp.dot(rows_factor, cols_factor, precision=HIGHEST)
    out_width = width // col_count
    child_out = lax.dynamic_slice_in_dim(rows_factor, col_id * out_width, out_width, 1).T

    strips = kernel_call(
        functools.partial(strips_kernel, (row_span, first, row_blocks)),
        "strips", (row_count, BLK, child_cols), 2, 1,
    )(ids, own_map, contribution)
    got = lax.all_to_all(strips, "row", 0, 0, tiled=True)
    tables = [pltpu.SMEM((count,), jnp.int32), pltpu.SMEM((cap,), jnp.int32)]
    tiles = kernel_call(
        functools.partial(
            tiles_kernel,
            (row_span, col_span, first, row_blocks, col_blocks, col_count, count),
        ),
        "tiles", (col_count, cap, BLK, BLK), 2, 1, tables,
    )(ids, own_map, got)
    landed = lax.all_to_all(
        tiles.reshape(col_count, cap * BLK, BLK), "col", 0, 0, tiled=True
    ).reshape(tiles.shape)
    other = kernel_call(
        functools.partial(other_kernel, (col_span, first, col_blocks, col_count, count)),
        "other", (col_span, cap, BLK, BLK), 2, 1,
    )(ids, own_map, landed)
    other = send(other, "leaf", swap)

    parent_order = parent_rows * row_count
    parent_width = parent_cols // 2
    assembled, diagonal, slab, top = kernel_call(
        functools.partial(
            assemble_kernel, (row_span, col_span, first, col_blocks, col_count, count)
        ),
        "assemble",
        [
            parent_front.shape, (parent_width, parent_width),
            (parent_rows, parent_width), (parent_width, parent_cols),
        ],
        3, 3, tables + [pltpu.SMEM((cap,), jnp.int32)],
    )(ids, own_map, partner_map, parent_front, other, landed)
    diagonal, slab, top = panel_parts(
        diagonal, slab, top, list(range(0, leaf_count, 2)), True
    )
    inverse = inverse_factor(diagonal)
    rows_factor = lax.dot_general(slab, inverse, (((1,), (1,)), ((), ())), precision=HIGHEST)
    cols_factor = jnp.dot(inverse, top, precision=HIGHEST)
    update = jnp.dot(rows_factor, cols_factor, precision=HIGHEST)
    row_ids = row_id * parent_rows + jnp.arange(parent_rows)
    col_ids = half_id * (parent_order // 2) + col_id * parent_cols + jnp.arange(parent_cols)
    keep = (row_ids[:, None] >= parent_width) & (col_ids[None, :] >= parent_width)
    parent_schur = jnp.where(keep, assembled - update, jnp.float32(0.0))
    share = parent_width // (2 * col_count)
    start = (half_id * col_count + col_id) * share
    parent_out = lax.dynamic_slice_in_dim(rows_factor, start, share, 1).T
    return (child_out[None], parent_out, parent_schur)


def solution(mesh):
    placed = (P("leaf", "row", "col"), P("row", ("leaf", "col")), P())
    return jax.shard_map(
        shards,
        mesh=mesh,
        in_specs=placed,
        out_specs=(P("leaf", "col", "row"), P(("leaf", "col"), "row"), P("row", ("leaf", "col"))),
        check_vma=False,
    )
```

```python
import functools

import jax
import jax.numpy as jnp
from jax import lax
from jax.experimental import pallas as pl
from jax.experimental.pallas import tpu as pltpu
from jax.sharding import PartitionSpec as P

BLK = 128
STEP = 64
GROUP = 8
HIGHEST = lax.Precision.HIGHEST


def send(value, axes, pairs):
    return lax.ppermute(value, axes, pairs)


HALVING = ([(0, 4)], [(0, 2), (4, 6)], [(0, 1), (2, 3), (4, 5), (6, 7)])


def reciprocal(x):
    guess = pltpu.reciprocal(x, approx=True)
    guess = guess * (2.0 - x * guess)
    return guess * (2.0 - x * guess)


def inverse_factor_kernel(a_ref, out_ref, x_ref):
    order = a_ref.shape[0]
    f32 = jnp.float32
    value = a_ref[...]
    full_sub = lax.broadcasted_iota(jnp.int32, value.shape, 0)
    full_lane = lax.broadcasted_iota(jnp.int32, value.shape, 1)
    diagonal = jnp.where(full_sub == full_lane, value, 0.0)
    scale_col = lax.rsqrt(jnp.sum(diagonal, axis=1, keepdims=True))
    scale_row = lax.rsqrt(jnp.sum(diagonal, axis=0, keepdims=True))
    x_ref[...] = (value * scale_col) * scale_row
    wide = (STEP, 2 * STEP)
    sub = lax.broadcasted_iota(jnp.int32, wide, 0)
    lane = lax.broadcasted_iota(jnp.int32, wide, 1)
    eye = (sub[:, :STEP] == lane[:, :STEP]).astype(f32)
    for start in range(0, order, STEP):
        stop = start + STEP
        rows = x_ref[start:stop, :]
        work = jnp.concatenate([x_ref[start:stop, start:stop], eye], axis=1)
        for base in range(0, STEP, GROUP):
            cols = [
                jnp.broadcast_to(work[:, base + j : base + j + 1], wide) for j in range(GROUP)
            ]
            for j in range(0, GROUP, 2):
                k = base + j
                c0, c1 = cols[j], cols[j + 1]
                p00, p01, p11 = c0[k : k + 1], c1[k : k + 1], c1[k + 1 : k + 2]
                over = reciprocal(p00 * p11 - p01 * p01)
                a00, a01, a11 = p00 * over, p01 * over, p11 * over
                below = sub > k + 1
                f0 = jnp.where(below, c0 * a11 - c1 * a01, 0.0)
                f1 = jnp.where(below, c1 * a00 - c0 * a01, 0.0)
                for i in range(j + 2, GROUP):
                    cols[i] = cols[i] - f0 * cols[i][k : k + 1] - f1 * cols[i][k + 1 : k + 2]
                work = work - f0 * work[k : k + 1] - f1 * work[k + 1 : k + 2]
        pivots = jnp.sum(jnp.where(sub == lane, work, 0.0), axis=1, keepdims=True)
        left = jnp.sum(jnp.where(sub == lane + 1, work, 0.0), axis=1, keepdims=True)
        above = pltpu.roll(jnp.broadcast_to(pivots, wide), 1, 0)
        work = work - jnp.where(sub % 2 == 1, left / above, 0.0) * pltpu.roll(work, 1, 0)
        pivots = jnp.sum(jnp.where(sub == lane, work, 0.0), axis=1, keepdims=True)
        inverse = work[:, STEP:] * lax.rsqrt(pivots)
        panel = jnp.dot(inverse, rows, precision=HIGHEST, preferred_element_type=f32)
        pieces = [inverse]
        if start:
            pieces.insert(0, panel[:, :start])
        if stop < order:
            pieces.append(panel[:, stop:])
        panel = jnp.concatenate(pieces, axis=1)
        x_ref[start:stop, :] = panel
        if stop < order:
            change = lax.dot_general(
                panel[:, stop:], panel, (((0,), (0,)), ((), ())),
                precision=HIGHEST, preferred_element_type=f32,
            )
            old = x_ref[stop:, :]
            at = lax.broadcasted_iota(jnp.int32, old.shape, 1)
            x_ref[stop:, :] = jnp.where((at >= start) & (at < stop), 0.0, old) - change
    out_ref[...] = jnp.where(full_lane <= full_sub, x_ref[...] * scale_row, 0.0)


def inverse_factor(block):
    return pl.pallas_call(
        inverse_factor_kernel,
        out_shape=jax.ShapeDtypeStruct(block.shape, jnp.float32),
        scratch_shapes=[pltpu.VMEM(block.shape, jnp.float32)],
        name="inverse_factor",
    )(block)


def smem():
    return pl.BlockSpec(memory_space=pltpu.SMEM)


def vmem():
    return pl.BlockSpec(memory_space=pltpu.VMEM)


def row_tables(map_ref, row, row_span, count, rank_ref, at_ref):
    for m in range(at_ref.shape[0]):
        at_ref[m] = -1

    def body(k, rank):
        here = map_ref[k] // row_span == row
        rank_ref[k] = jnp.where(here, rank, -1)

        @pl.when(here)
        def _():
            at_ref[jnp.minimum(rank, at_ref.shape[0] - 1)] = map_ref[k] % row_span

        return rank + here.astype(jnp.int32)

    lax.fori_loop(0, count, body, jnp.int32(0))


def strips_kernel(sizes, ids_ref, map_ref, part_ref, out_ref):
    row_span, first, row_blocks = sizes
    row = ids_ref[1]
    for a in range(row_blocks):
        block = row * row_blocks + a - first

        @pl.when(block >= 0)
        def _():
            target = map_ref[jnp.maximum(block, 0)] // row_span
            out_ref[target] = part_ref[a * BLK : (a + 1) * BLK, :]


def tiles_kernel(sizes, ids_ref, map_ref, got_ref, out_ref, rank_ref, at_ref):
    row_span, col_span, first, row_blocks, col_blocks, cols, count = sizes
    row, col = ids_ref[1], ids_ref[2]
    row_tables(map_ref, row, row_span, count, rank_ref, at_ref)

    def body(k, carry):
        rank = rank_ref[k]

        @pl.when(rank >= 0)
        def _():
            source = (k + first) // row_blocks
            slot = jnp.minimum(rank, out_ref.shape[1] - 1)
            for y in range(col_blocks):
                block = col * col_blocks + y - first

                @pl.when(block >= 0)
                def _():
                    target = (map_ref[jnp.maximum(block, 0)] // col_span) % cols
                    out_ref[target, slot] = got_ref[source, :, y * BLK : (y + 1) * BLK]

        return carry

    lax.fori_loop(0, count, body, jnp.int32(0))


def other_kernel(sizes, ids_ref, map_ref, landed_ref, out_ref):
    col_span, first, col_blocks, cols, count = sizes
    half, col = ids_ref[0], ids_ref[2]
    out_ref[...] = jnp.zeros_like(out_ref)

    def body(k, carry):
        owner = map_ref[k] // col_span

        @pl.when((owner % cols == col) & (owner // cols != half))
        def _():
            out_ref[map_ref[k] % col_span] = landed_ref[(k + first) // col_blocks]

        return carry

    lax.fori_loop(0, count, body, jnp.int32(0))


def assemble_kernel(sizes, ids_ref, map_ref, pair_map_ref, parent_ref, other_ref, landed_ref,
                    out_ref, diagonal_ref, slab_ref, top_ref, rank_ref, at_ref, pair_at_ref):
    row_span, col_span, first, col_blocks, cols, count = sizes
    half, row, col = ids_ref[0], ids_ref[1], ids_ref[2]
    out_ref[...] = parent_ref[...].astype(jnp.float32)
    row_tables(pair_map_ref, row, row_span, count, rank_ref, pair_at_ref)
    row_tables(map_ref, row, row_span, count, rank_ref, at_ref)
    caps = at_ref.shape[0]
    for m in range(caps):
        at = pair_at_ref[m]

        @pl.when(at >= 0)
        def _():
            for y in range(col_span):
                spot = (
                    pl.ds(pl.multiple_of(at * BLK, BLK), BLK), slice(y * BLK, (y + 1) * BLK)
                )
                out_ref[spot] = out_ref[spot] + other_ref[y, m]

    def body(k, carry):
        owner = map_ref[k] // col_span

        @pl.when((owner % cols == col) & (owner // cols == half))
        def _():
            at_col = pl.ds(pl.multiple_of((map_ref[k] % col_span) * BLK, BLK), BLK)
            for m in range(caps):
                at = at_ref[m]

                @pl.when(at >= 0)
                def _():
                    spot = (pl.ds(pl.multiple_of(at * BLK, BLK), BLK), at_col)
                    out_ref[spot] = out_ref[spot] + landed_ref[(k + first) // col_blocks, m]

        return carry

    lax.fori_loop(0, count, body, jnp.int32(0))
    width = diagonal_ref.shape[0]
    diagonal_ref[...] = out_ref[:width, :width]
    slab_ref[...] = out_ref[:, :width]
    top_ref[...] = out_ref[:width, :]


def kernel_call(body, name, outs, n_smem, n_vmem, scratch=()):
    many = isinstance(outs, list)
    shapes = [jax.ShapeDtypeStruct(o, jnp.float32) for o in (outs if many else [outs])]
    specs = [vmem() for _ in shapes]
    return pl.pallas_call(
        body,
        out_shape=shapes if many else shapes[0],
        in_specs=[smem()] * n_smem + [vmem()] * n_vmem,
        out_specs=specs if many else specs[0],
        scratch_shapes=list(scratch),
        compiler_params=pltpu.CompilerParams(vmem_limit_bytes=40 * 2**20),
        name=name,
    )


def shards(child_front, parent_front, block_map):
    leaf_id = lax.axis_index("leaf")
    row_id = lax.axis_index("row")
    col_id = lax.axis_index("col")
    row_count = lax.axis_size("row")
    col_count = lax.axis_size("col")
    leaf_count = lax.axis_size("leaf")
    half_id = leaf_id % 2
    ids = jnp.stack([half_id, row_id, col_id]).astype(jnp.int32)
    own_map = lax.dynamic_index_in_dim(block_map, leaf_id, 0, keepdims=False)
    partner_map = lax.dynamic_index_in_dim(block_map, leaf_id ^ 1, 0, keepdims=False)
    count = own_map.shape[0]

    child_block = child_front[0]
    child_rows, child_cols = child_block.shape
    width = child_cols // 2
    parent_rows, parent_cols = parent_front.shape
    row_span, col_span = parent_rows // BLK, parent_cols // BLK
    row_blocks, col_blocks = child_rows // BLK, child_cols // BLK
    first = width // BLK
    cap = -(-count // row_count)
    swap = [(i, i ^ 1) for i in range(leaf_count)]

    def only(axis, got, value, targets):
        index = lax.axis_index(axis)
        hit = functools.reduce(jnp.logical_or, [index == t for t in targets])
        return jnp.where(hit, got, value)

    def after(value, earlier):
        return lax.optimization_barrier((value, earlier))[0]

    grid = row_count * col_count
    fan = list(range(2, row_count, 2))

    def panel_parts(diagonal, slab, top, leaves, paired):
        def first_row(value, pairs):
            moves = [(l * grid + r, l * grid + q) for l in leaves for r, q in pairs]
            got = send(value, ("leaf", "row", "col"), moves)
            return only("col", got, value, [q for _, q in pairs])

        def down(value, pairs):
            moves = [(l * row_count + r, l * row_count + q) for l in leaves for r, q in pairs]
            return send(value, ("leaf", "row"), moves)

        def along(value, pairs):
            moves = [(l * col_count + r, l * col_count + q) for l in leaves for r, q in pairs]
            got = send(value, ("leaf", "col"), moves)
            return only("col", got, value, [q for _, q in pairs])

        def over(value, pairs):
            return only("row", send(value, "row", pairs), value, [q for _, q in pairs])

        d1 = first_row(diagonal, HALVING[0])
        slab1 = along(slab, HALVING[0])
        top1 = over(top, [(0, 1)])
        d2 = first_row(d1, HALVING[1])
        slab2 = along(after(slab1, d1), HALVING[1])
        top2 = over(after(top1, d1), [(0, 4), (1, 5)])
        d3 = first_row(d2, HALVING[2])
        slab3 = along(after(slab2, d2), HALVING[2])
        top3 = over(after(top2, d2), [(0, 2), (1, 3), (4, 6), (5, 7)])
        d4 = only("row", down(d3, [(0, 1)]), d3, [1])
        hops = [[(0, q), (1, q + 1)] for q in fan]
        d5 = functools.reduce(jnp.add, [down(d4, pairs) for pairs in hops])
        d5 = only("row", d5, d4, [q for pairs in hops for _, q in pairs])
        if paired:
            across = [(l, l + 1) for l in leaves]
            d5 = jnp.where(half_id == 0, d5, send(d5, "leaf", across))
            slab3 = jnp.where(half_id == 0, slab3, send(slab3, "leaf", across))
        return d5, slab3, top3

    diagonal, slab, top = panel_parts(
        child_block[:width, :width], child_block[:, :width], child_block[:width],
        list(range(leaf_count)), False,
    )
    inverse = inverse_factor(diagonal)
    rows_factor = lax.dot_general(slab, inverse, (((1,), (1,)), ((), ())), precision=HIGHEST)
    cols_factor = jnp.dot(inverse, top, precision=HIGHEST)
    contribution = child_block - jnp.dot(rows_factor, cols_factor, precision=HIGHEST)
    out_width = width // col_count
    child_out = lax.dynamic_slice_in_dim(rows_factor, col_id * out_width, out_width, 1).T

    strips = kernel_call(
        functools.partial(strips_kernel, (row_span, first, row_blocks)),
        "strips", (row_count, BLK, child_cols), 2, 1,
    )(ids, own_map, contribution)
    got = lax.all_to_all(strips, "row", 0, 0, tiled=True)
    tables = [pltpu.SMEM((count,), jnp.int32), pltpu.SMEM((cap,), jnp.int32)]
    tiles = kernel_call(
        functools.partial(
            tiles_kernel,
            (row_span, col_span, first, row_blocks, col_blocks, col_count, count),
        ),
        "tiles", (col_count, cap, BLK, BLK), 2, 1, tables,
    )(ids, own_map, got)
    landed = lax.all_to_all(
        tiles.reshape(col_count, cap * BLK, BLK), "col", 0, 0, tiled=True
    ).reshape(tiles.shape)
    other = kernel_call(
        functools.partial(other_kernel, (col_span, first, col_blocks, col_count, count)),
        "other", (col_span, cap, BLK, BLK), 2, 1,
    )(ids, own_map, landed)
    other = send(other, "leaf", swap)

    parent_order = parent_rows * row_count
    parent_width = parent_cols // 2
    assembled, diagonal, slab, top = kernel_call(
        functools.partial(
            assemble_kernel, (row_span, col_span, first, col_blocks, col_count, count)
        ),
        "assemble",
        [
            parent_front.shape, (parent_width, parent_width),
            (parent_rows, parent_width), (parent_width, parent_cols),
        ],
        3, 3, tables + [pltpu.SMEM((cap,), jnp.int32)],
    )(ids, own_map, partner_map, parent_front, other, landed)
    diagonal, slab, top = panel_parts(
        diagonal, slab, top, list(range(0, leaf_count, 2)), True
    )
    inverse = inverse_factor(diagonal)
    rows_factor = lax.dot_general(slab, inverse, (((1,), (1,)), ((), ())), precision=HIGHEST)
    cols_factor = jnp.dot(inverse, top, precision=HIGHEST)
    update = jnp.dot(rows_factor, cols_factor, precision=HIGHEST)
    row_ids = row_id * parent_rows + jnp.arange(parent_rows)
    col_ids = half_id * (parent_order // 2) + col_id * parent_cols + jnp.arange(parent_cols)
    keep = (row_ids[:, None] >= parent_width) & (col_ids[None, :] >= parent_width)
    parent_schur = jnp.where(keep, assembled - update, jnp.float32(0.0))
    share = parent_width // (2 * col_count)
    start = (half_id * col_count + col_id) * share
    parent_out = lax.dynamic_slice_in_dim(rows_factor, start, share, 1).T
    return (child_out[None], parent_out, parent_schur)


def solution(mesh):
    placed = (P("leaf", "row", "col"), P("row", ("leaf", "col")), P())
    return jax.shard_map(
        shards,
        mesh=mesh,
        in_specs=placed,
        out_specs=(P("leaf", "col", "row"), P(("leaf", "col"), "row"), P("row", ("leaf", "col"))),
        check_vma=False,
    )
```

```python
import functools

import jax
import jax.numpy as jnp
from jax import lax
from jax.experimental import pallas as pl
from jax.experimental.pallas import tpu as pltpu
from jax.sharding import PartitionSpec as P

BLK = 128
STEP = 64
GROUP = 8
HIGHEST = lax.Precision.HIGHEST


def send(value, axes, pairs):
    return lax.ppermute(value, axes, pairs)


HALVING = ([(0, 4)], [(0, 2), (4, 6)], [(0, 1), (2, 3), (4, 5), (6, 7)])


def reciprocal(x):
    guess = pltpu.reciprocal(x, approx=True)
    guess = guess * (2.0 - x * guess)
    return guess * (2.0 - x * guess)


def inverse_factor_kernel(a_ref, out_ref, x_ref):
    order = a_ref.shape[0]
    f32 = jnp.float32
    value = a_ref[...]
    full_sub = lax.broadcasted_iota(jnp.int32, value.shape, 0)
    full_lane = lax.broadcasted_iota(jnp.int32, value.shape, 1)
    diagonal = jnp.where(full_sub == full_lane, value, 0.0)
    scale_col = lax.rsqrt(jnp.sum(diagonal, axis=1, keepdims=True))
    scale_row = lax.rsqrt(jnp.sum(diagonal, axis=0, keepdims=True))
    x_ref[...] = (value * scale_col) * scale_row
    wide = (STEP, 2 * STEP)
    sub = lax.broadcasted_iota(jnp.int32, wide, 0)
    lane = lax.broadcasted_iota(jnp.int32, wide, 1)
    eye = (sub[:, :STEP] == lane[:, :STEP]).astype(f32)
    for start in range(0, order, STEP):
        stop = start + STEP
        rows = x_ref[start:stop, :]
        work = jnp.concatenate([x_ref[start:stop, start:stop], eye], axis=1)
        for base in range(0, STEP, GROUP):
            cols = [
                jnp.broadcast_to(work[:, base + j : base + j + 1], wide) for j in range(GROUP)
            ]
            for j in range(0, GROUP, 2):
                k = base + j
                c0, c1 = cols[j], cols[j + 1]
                p00, p01, p11 = c0[k : k + 1], c1[k : k + 1], c1[k + 1 : k + 2]
                over = reciprocal(p00 * p11 - p01 * p01)
                a00, a01, a11 = p00 * over, p01 * over, p11 * over
                below = sub > k + 1
                f0 = jnp.where(below, c0 * a11 - c1 * a01, 0.0)
                f1 = jnp.where(below, c1 * a00 - c0 * a01, 0.0)
                for i in range(j + 2, GROUP):
                    cols[i] = cols[i] - f0 * cols[i][k : k + 1] - f1 * cols[i][k + 1 : k + 2]
                work = work - f0 * work[k : k + 1] - f1 * work[k + 1 : k + 2]
        pivots = jnp.sum(jnp.where(sub == lane, work, 0.0), axis=1, keepdims=True)
        left = jnp.sum(jnp.where(sub == lane + 1, work, 0.0), axis=1, keepdims=True)
        above = pltpu.roll(jnp.broadcast_to(pivots, wide), 1, 0)
        work = work - jnp.where(sub % 2 == 1, left / above, 0.0) * pltpu.roll(work, 1, 0)
        pivots = jnp.sum(jnp.where(sub == lane, work, 0.0), axis=1, keepdims=True)
        inverse = work[:, STEP:] * lax.rsqrt(pivots)
        panel = jnp.dot(inverse, rows, precision=HIGHEST, preferred_element_type=f32)
        pieces = [inverse]
        if start:
            pieces.insert(0, panel[:, :start])
        if stop < order:
            pieces.append(panel[:, stop:])
        panel = jnp.concatenate(pieces, axis=1)
        x_ref[start:stop, :] = panel
        if stop < order:
            change = lax.dot_general(
                panel[:, stop:], panel, (((0,), (0,)), ((), ())),
                precision=HIGHEST, preferred_element_type=f32,
            )
            old = x_ref[stop:, :]
            at = lax.broadcasted_iota(jnp.int32, old.shape, 1)
            x_ref[stop:, :] = jnp.where((at >= start) & (at < stop), 0.0, old) - change
    out_ref[...] = jnp.where(full_lane <= full_sub, x_ref[...] * scale_row, 0.0)


def inverse_factor(block):
    return pl.pallas_call(
        inverse_factor_kernel,
        out_shape=jax.ShapeDtypeStruct(block.shape, jnp.float32),
        scratch_shapes=[pltpu.VMEM(block.shape, jnp.float32)],
        name="inverse_factor",
    )(block)


def smem():
    return pl.BlockSpec(memory_space=pltpu.SMEM)


def vmem():
    return pl.BlockSpec(memory_space=pltpu.VMEM)


def row_tables(map_ref, row, row_span, count, rank_ref, at_ref):
    for m in range(at_ref.shape[0]):
        at_ref[m] = -1

    def body(k, rank):
        here = map_ref[k] // row_span == row
        rank_ref[k] = jnp.where(here, rank, -1)

        @pl.when(here)
        def _():
            at_ref[jnp.minimum(rank, at_ref.shape[0] - 1)] = map_ref[k] % row_span

        return rank + here.astype(jnp.int32)

    lax.fori_loop(0, count, body, jnp.int32(0))


def strips_kernel(sizes, ids_ref, map_ref, part_ref, out_ref):
    row_span, first, row_blocks = sizes
    row = ids_ref[1]
    for a in range(row_blocks):
        block = row * row_blocks + a - first

        @pl.when(block >= 0)
        def _():
            target = map_ref[jnp.maximum(block, 0)] // row_span
            out_ref[target] = part_ref[a * BLK : (a + 1) * BLK, :]


def tiles_kernel(sizes, ids_ref, map_ref, got_ref, out_ref, rank_ref, at_ref):
    row_span, col_span, first, row_blocks, col_blocks, cols, count = sizes
    row, col = ids_ref[1], ids_ref[2]
    row_tables(map_ref, row, row_span, count, rank_ref, at_ref)

    def body(k, carry):
        rank = rank_ref[k]

        @pl.when(rank >= 0)
        def _():
            source = (k + first) // row_blocks
            slot = jnp.minimum(rank, out_ref.shape[1] - 1)
            for y in range(col_blocks):
                block = col * col_blocks + y - first

                @pl.when(block >= 0)
                def _():
                    target = (map_ref[jnp.maximum(block, 0)] // col_span) % cols
                    out_ref[target, slot] = got_ref[source, :, y * BLK : (y + 1) * BLK]

        return carry

    lax.fori_loop(0, count, body, jnp.int32(0))


def other_kernel(sizes, ids_ref, map_ref, landed_ref, out_ref):
    col_span, first, col_blocks, cols, count = sizes
    half, col = ids_ref[0], ids_ref[2]
    out_ref[...] = jnp.zeros_like(out_ref)

    def body(k, carry):
        owner = map_ref[k] // col_span

        @pl.when((owner % cols == col) & (owner // cols != half))
        def _():
            out_ref[map_ref[k] % col_span] = landed_ref[(k + first) // col_blocks]

        return carry

    lax.fori_loop(0, count, body, jnp.int32(0))


def assemble_kernel(sizes, ids_ref, map_ref, pair_map_ref, parent_ref, other_ref, landed_ref,
                    out_ref, diagonal_ref, slab_ref, top_ref, rank_ref, at_ref, pair_at_ref):
    row_span, col_span, first, col_blocks, cols, count = sizes
    half, row, col = ids_ref[0], ids_ref[1], ids_ref[2]
    out_ref[...] = parent_ref[...].astype(jnp.float32)
    row_tables(pair_map_ref, row, row_span, count, rank_ref, pair_at_ref)
    row_tables(map_ref, row, row_span, count, rank_ref, at_ref)
    caps = at_ref.shape[0]
    for m in range(caps):
        at = pair_at_ref[m]

        @pl.when(at >= 0)
        def _():
            for y in range(col_span):
                spot = (
                    pl.ds(pl.multiple_of(at * BLK, BLK), BLK), slice(y * BLK, (y + 1) * BLK)
                )
                out_ref[spot] = out_ref[spot] + other_ref[y, m]

    def body(k, carry):
        owner = map_ref[k] // col_span

        @pl.when((owner % cols == col) & (owner // cols == half))
        def _():
            at_col = pl.ds(pl.multiple_of((map_ref[k] % col_span) * BLK, BLK), BLK)
            for m in range(caps):
                at = at_ref[m]

                @pl.when(at >= 0)
                def _():
                    spot = (pl.ds(pl.multiple_of(at * BLK, BLK), BLK), at_col)
                    out_ref[spot] = out_ref[spot] + landed_ref[(k + first) // col_blocks, m]

        return carry

    lax.fori_loop(0, count, body, jnp.int32(0))
    width = diagonal_ref.shape[0]
    diagonal_ref[...] = out_ref[:width, :width]
    slab_ref[...] = out_ref[:, :width]
    top_ref[...] = out_ref[:width, :]


def kernel_call(body, name, outs, n_smem, n_vmem, scratch=()):
    many = isinstance(outs, list)
    shapes = [jax.ShapeDtypeStruct(o, jnp.float32) for o in (outs if many else [outs])]
    specs = [vmem() for _ in shapes]
    return pl.pallas_call(
        body,
        out_shape=shapes if many else shapes[0],
        in_specs=[smem()] * n_smem + [vmem()] * n_vmem,
        out_specs=specs if many else specs[0],
        scratch_shapes=list(scratch),
        compiler_params=pltpu.CompilerParams(vmem_limit_bytes=40 * 2**20),
        name=name,
    )


def shards(child_front, parent_front, block_map):
    leaf_id = lax.axis_index("leaf")
    row_id = lax.axis_index("row")
    col_id = lax.axis_index("col")
    row_count = lax.axis_size("row")
    col_count = lax.axis_size("col")
    leaf_count = lax.axis_size("leaf")
    half_id = leaf_id % 2
    ids = jnp.stack([half_id, row_id, col_id]).astype(jnp.int32)
    own_map = lax.dynamic_index_in_dim(block_map, leaf_id, 0, keepdims=False)
    partner_map = lax.dynamic_index_in_dim(block_map, leaf_id ^ 1, 0, keepdims=False)
    count = own_map.shape[0]

    child_block = child_front[0]
    child_rows, child_cols = child_block.shape
    width = child_cols // 2
    parent_rows, parent_cols = parent_front.shape
    row_span, col_span = parent_rows // BLK, parent_cols // BLK
    row_blocks, col_blocks = child_rows // BLK, child_cols // BLK
    first = width // BLK
    cap = -(-count // row_count)
    swap = [(i, i ^ 1) for i in range(leaf_count)]

    def only(axis, got, value, targets):
        index = lax.axis_index(axis)
        hit = functools.reduce(jnp.logical_or, [index == t for t in targets])
        return jnp.where(hit, got, value)

    def after(value, earlier):
        return lax.optimization_barrier((value, earlier))[0]

    grid = row_count * col_count

    def panel_parts(diagonal, slab, top, leaves, paired):
        def down(value, pairs):
            moves = [
                (l * grid + r * col_count, l * grid + q * col_count)
                for l in leaves for r, q in pairs
            ]
            return send(value, ("leaf", "row", "col"), moves)

        def along(value, pairs):
            moves = [(l * col_count + r, l * col_count + q) for l in leaves for r, q in pairs]
            got = send(value, ("leaf", "col"), moves)
            return only("col", got, value, [q for _, q in pairs])

        def over(value, pairs):
            return send(value, "row", pairs)

        def joined(value, bit):
            got = over(value, [(r, r ^ bit) for r in range(row_count)])
            upper = (row_id // bit) % 2 == 1
            return jnp.concatenate(
                [jnp.where(upper, got, value), jnp.where(upper, value, got)], axis=0
            )

        fan = list(range(2, row_count, 2))
        d1 = functools.reduce(jnp.add, [down(diagonal, [(0, q)]) for q in fan])
        d1 = only("row", d1, diagonal, fan)
        slab1 = along(slab, HALVING[0])
        size = top.shape[0] // 2
        half = only("row", over(top[size:], [(0, 4)]), top[:size], [4])
        zhi = [(r, r + 1) for r in range(0, row_count, 2)]
        d2 = only("row", down(d1, zhi), d1, [q for _, q in zhi])
        half = after(half, d1)
        size = size // 2
        part = only("row", over(half[size:], [(0, 2), (4, 6)]), half[:size], [2, 6])
        d3 = along(d2, HALVING[0])
        slab2 = along(after(slab1, d2), HALVING[1])
        part = after(part, d2)
        part = only("row", over(part, zhi), part, [q for _, q in zhi])
        d4 = along(d3, HALVING[1])
        slab3 = along(after(slab2, d3), HALVING[2])
        part = joined(after(part, d3), 2)
        d5 = along(d4, HALVING[2])
        top3 = joined(after(part, d4), 4)
        if paired:
            across = [(l, l + 1) for l in leaves]
            d5 = jnp.where(half_id == 0, d5, send(d5, "leaf", across))
            slab3 = jnp.where(half_id == 0, slab3, send(slab3, "leaf", across))
        return d5, slab3, top3

    diagonal, slab, top = panel_parts(
        child_block[:width, :width], child_block[:, :width], child_block[:width],
        list(range(leaf_count)), False,
    )
    inverse = inverse_factor(diagonal)
    rows_factor = lax.dot_general(slab, inverse, (((1,), (1,)), ((), ())), precision=HIGHEST)
    cols_factor = jnp.dot(inverse, top, precision=HIGHEST)
    contribution = child_block - jnp.dot(rows_factor, cols_factor, precision=HIGHEST)
    out_width = width // col_count
    child_out = lax.dynamic_slice_in_dim(rows_factor, col_id * out_width, out_width, 1).T

    strips = kernel_call(
        functools.partial(strips_kernel, (row_span, first, row_blocks)),
        "strips", (row_count, BLK, child_cols), 2, 1,
    )(ids, own_map, contribution)
    got = lax.all_to_all(strips, "row", 0, 0, tiled=True)
    tables = [pltpu.SMEM((count,), jnp.int32), pltpu.SMEM((cap,), jnp.int32)]
    tiles = kernel_call(
        functools.partial(
            tiles_kernel,
            (row_span, col_span, first, row_blocks, col_blocks, col_count, count),
        ),
        "tiles", (col_count, cap, BLK, BLK), 2, 1, tables,
    )(ids, own_map, got)
    landed = lax.all_to_all(
        tiles.reshape(col_count, cap * BLK, BLK), "col", 0, 0, tiled=True
    ).reshape(tiles.shape)
    other = kernel_call(
        functools.partial(other_kernel, (col_span, first, col_blocks, col_count, count)),
        "other", (col_span, cap, BLK, BLK), 2, 1,
    )(ids, own_map, landed)
    other = send(other, "leaf", swap)

    parent_order = parent_rows * row_count
    parent_width = parent_cols // 2
    assembled, diagonal, slab, top = kernel_call(
        functools.partial(
            assemble_kernel, (row_span, col_span, first, col_blocks, col_count, count)
        ),
        "assemble",
        [
            parent_front.shape, (parent_width, parent_width),
            (parent_rows, parent_width), (parent_width, parent_cols),
        ],
        3, 3, tables + [pltpu.SMEM((cap,), jnp.int32)],
    )(ids, own_map, partner_map, parent_front, other, landed)
    diagonal, slab, top = panel_parts(
        diagonal, slab, top, list(range(0, leaf_count, 2)), True
    )
    inverse = inverse_factor(diagonal)
    rows_factor = lax.dot_general(slab, inverse, (((1,), (1,)), ((), ())), precision=HIGHEST)
    cols_factor = jnp.dot(inverse, top, precision=HIGHEST)
    update = jnp.dot(rows_factor, cols_factor, precision=HIGHEST)
    row_ids = row_id * parent_rows + jnp.arange(parent_rows)
    col_ids = half_id * (parent_order // 2) + col_id * parent_cols + jnp.arange(parent_cols)
    keep = (row_ids[:, None] >= parent_width) & (col_ids[None, :] >= parent_width)
    parent_schur = jnp.where(keep, assembled - update, jnp.float32(0.0))
    share = parent_width // (2 * col_count)
    start = (half_id * col_count + col_id) * share
    parent_out = lax.dynamic_slice_in_dim(rows_factor, start, share, 1).T
    return (child_out[None], parent_out, parent_schur)


def solution(mesh):
    placed = (P("leaf", "row", "col"), P("row", ("leaf", "col")), P())
    return jax.shard_map(
        shards,
        mesh=mesh,
        in_specs=placed,
        out_specs=(P("leaf", "col", "row"), P(("leaf", "col"), "row"), P("row", ("leaf", "col"))),
        check_vma=False,
    )
```

```python
import functools

import jax
import jax.numpy as jnp
from jax import lax
from jax.experimental import pallas as pl
from jax.experimental.pallas import tpu as pltpu
from jax.sharding import PartitionSpec as P

BLK = 128
STEP = 64
GROUP = 8
HIGHEST = lax.Precision.HIGHEST


def send(value, axes, pairs):
    return lax.ppermute(value, axes, pairs)


HALVING = ([(0, 4)], [(0, 2), (4, 6)], [(0, 1), (2, 3), (4, 5), (6, 7)])


def reciprocal(x):
    guess = pltpu.reciprocal(x, approx=True)
    guess = guess * (2.0 - x * guess)
    return guess * (2.0 - x * guess)


def inverse_factor_kernel(a_ref, out_ref, x_ref):
    order = a_ref.shape[0]
    f32 = jnp.float32
    value = a_ref[...]
    full_sub = lax.broadcasted_iota(jnp.int32, value.shape, 0)
    full_lane = lax.broadcasted_iota(jnp.int32, value.shape, 1)
    diagonal = jnp.where(full_sub == full_lane, value, 0.0)
    scale_col = lax.rsqrt(jnp.sum(diagonal, axis=1, keepdims=True))
    scale_row = lax.rsqrt(jnp.sum(diagonal, axis=0, keepdims=True))
    x_ref[...] = (value * scale_col) * scale_row
    wide = (STEP, 2 * STEP)
    sub = lax.broadcasted_iota(jnp.int32, wide, 0)
    lane = lax.broadcasted_iota(jnp.int32, wide, 1)
    eye = (sub[:, :STEP] == lane[:, :STEP]).astype(f32)
    for start in range(0, order, STEP):
        stop = start + STEP
        rows = x_ref[start:stop, :]
        work = jnp.concatenate([x_ref[start:stop, start:stop], eye], axis=1)
        for base in range(0, STEP, GROUP):
            cols = [
                jnp.broadcast_to(work[:, base + j : base + j + 1], wide) for j in range(GROUP)
            ]
            for j in range(0, GROUP, 2):
                k = base + j
                c0, c1 = cols[j], cols[j + 1]
                p00, p01, p11 = c0[k : k + 1], c1[k : k + 1], c1[k + 1 : k + 2]
                over = reciprocal(p00 * p11 - p01 * p01)
                a00, a01, a11 = p00 * over, p01 * over, p11 * over
                below = sub > k + 1
                f0 = jnp.where(below, c0 * a11 - c1 * a01, 0.0)
                f1 = jnp.where(below, c1 * a00 - c0 * a01, 0.0)
                for i in range(j + 2, GROUP):
                    cols[i] = cols[i] - f0 * cols[i][k : k + 1] - f1 * cols[i][k + 1 : k + 2]
                work = work - f0 * work[k : k + 1] - f1 * work[k + 1 : k + 2]
        pivots = jnp.sum(jnp.where(sub == lane, work, 0.0), axis=1, keepdims=True)
        left = jnp.sum(jnp.where(sub == lane + 1, work, 0.0), axis=1, keepdims=True)
        above = pltpu.roll(jnp.broadcast_to(pivots, wide), 1, 0)
        work = work - jnp.where(sub % 2 == 1, left / above, 0.0) * pltpu.roll(work, 1, 0)
        pivots = jnp.sum(jnp.where(sub == lane, work, 0.0), axis=1, keepdims=True)
        inverse = work[:, STEP:] * lax.rsqrt(pivots)
        panel = jnp.dot(inverse, rows, precision=HIGHEST, preferred_element_type=f32)
        pieces = [inverse]
        if start:
            pieces.insert(0, panel[:, :start])
        if stop < order:
            pieces.append(panel[:, stop:])
        panel = jnp.concatenate(pieces, axis=1)
        x_ref[start:stop, :] = panel
        if stop < order:
            change = lax.dot_general(
                panel[:, stop:], panel, (((0,), (0,)), ((), ())),
                precision=HIGHEST, preferred_element_type=f32,
            )
            old = x_ref[stop:, :]
            at = lax.broadcasted_iota(jnp.int32, old.shape, 1)
            x_ref[stop:, :] = jnp.where((at >= start) & (at < stop), 0.0, old) - change
    out_ref[...] = jnp.where(full_lane <= full_sub, x_ref[...] * scale_row, 0.0)


def inverse_factor(block):
    return pl.pallas_call(
        inverse_factor_kernel,
        out_shape=jax.ShapeDtypeStruct(block.shape, jnp.float32),
        scratch_shapes=[pltpu.VMEM(block.shape, jnp.float32)],
        name="inverse_factor",
    )(block)


def smem():
    return pl.BlockSpec(memory_space=pltpu.SMEM)


def vmem():
    return pl.BlockSpec(memory_space=pltpu.VMEM)


def row_tables(map_ref, row, row_span, count, rank_ref, at_ref):
    for m in range(at_ref.shape[0]):
        at_ref[m] = -1

    def body(k, rank):
        here = map_ref[k] // row_span == row
        rank_ref[k] = jnp.where(here, rank, -1)

        @pl.when(here)
        def _():
            at_ref[jnp.minimum(rank, at_ref.shape[0] - 1)] = map_ref[k] % row_span

        return rank + here.astype(jnp.int32)

    lax.fori_loop(0, count, body, jnp.int32(0))


def strips_kernel(sizes, ids_ref, map_ref, part_ref, out_ref):
    row_span, first, row_blocks = sizes
    row = ids_ref[1]
    for a in range(row_blocks):
        block = row * row_blocks + a - first

        @pl.when(block >= 0)
        def _():
            target = map_ref[jnp.maximum(block, 0)] // row_span
            out_ref[target] = part_ref[a * BLK : (a + 1) * BLK, :]


def tiles_kernel(sizes, ids_ref, map_ref, got_ref, out_ref, rank_ref, at_ref):
    row_span, col_span, first, row_blocks, col_blocks, cols, count = sizes
    row, col = ids_ref[1], ids_ref[2]
    row_tables(map_ref, row, row_span, count, rank_ref, at_ref)

    def body(k, carry):
        rank = rank_ref[k]

        @pl.when(rank >= 0)
        def _():
            source = (k + first) // row_blocks
            slot = jnp.minimum(rank, out_ref.shape[1] - 1)
            for y in range(col_blocks):
                block = col * col_blocks + y - first

                @pl.when(block >= 0)
                def _():
                    target = (map_ref[jnp.maximum(block, 0)] // col_span) % cols
                    out_ref[target, slot] = got_ref[source, :, y * BLK : (y + 1) * BLK]

        return carry

    lax.fori_loop(0, count, body, jnp.int32(0))


def other_kernel(sizes, ids_ref, map_ref, landed_ref, out_ref):
    col_span, first, col_blocks, cols, count = sizes
    half, col = ids_ref[0], ids_ref[2]
    out_ref[...] = jnp.zeros_like(out_ref)

    def body(k, carry):
        owner = map_ref[k] // col_span

        @pl.when((owner % cols == col) & (owner // cols != half))
        def _():
            out_ref[map_ref[k] % col_span] = landed_ref[(k + first) // col_blocks]

        return carry

    lax.fori_loop(0, count, body, jnp.int32(0))


def assemble_kernel(sizes, ids_ref, map_ref, pair_map_ref, parent_ref, other_ref, landed_ref,
                    out_ref, diagonal_ref, slab_ref, top_ref, rank_ref, at_ref, pair_at_ref):
    row_span, col_span, first, col_blocks, cols, count = sizes
    half, row, col = ids_ref[0], ids_ref[1], ids_ref[2]
    out_ref[...] = parent_ref[...].astype(jnp.float32)
    row_tables(pair_map_ref, row, row_span, count, rank_ref, pair_at_ref)
    row_tables(map_ref, row, row_span, count, rank_ref, at_ref)
    caps = at_ref.shape[0]
    for m in range(caps):
        at = pair_at_ref[m]

        @pl.when(at >= 0)
        def _():
            for y in range(col_span):
                spot = (
                    pl.ds(pl.multiple_of(at * BLK, BLK), BLK), slice(y * BLK, (y + 1) * BLK)
                )
                out_ref[spot] = out_ref[spot] + other_ref[y, m]

    def body(k, carry):
        owner = map_ref[k] // col_span

        @pl.when((owner % cols == col) & (owner // cols == half))
        def _():
            at_col = pl.ds(pl.multiple_of((map_ref[k] % col_span) * BLK, BLK), BLK)
            for m in range(caps):
                at = at_ref[m]

                @pl.when(at >= 0)
                def _():
                    spot = (pl.ds(pl.multiple_of(at * BLK, BLK), BLK), at_col)
                    out_ref[spot] = out_ref[spot] + landed_ref[(k + first) // col_blocks, m]

        return carry

    lax.fori_loop(0, count, body, jnp.int32(0))
    width = diagonal_ref.shape[0]
    diagonal_ref[...] = out_ref[:width, :width]
    slab_ref[...] = out_ref[:, :width]
    top_ref[...] = out_ref[:width, :]


def kernel_call(body, name, outs, n_smem, n_vmem, scratch=()):
    many = isinstance(outs, list)
    shapes = [jax.ShapeDtypeStruct(o, jnp.float32) for o in (outs if many else [outs])]
    specs = [vmem() for _ in shapes]
    return pl.pallas_call(
        body,
        out_shape=shapes if many else shapes[0],
        in_specs=[smem()] * n_smem + [vmem()] * n_vmem,
        out_specs=specs if many else specs[0],
        scratch_shapes=list(scratch),
        compiler_params=pltpu.CompilerParams(vmem_limit_bytes=40 * 2**20),
        name=name,
    )


def shards(child_front, parent_front, block_map):
    leaf_id = lax.axis_index("leaf")
    row_id = lax.axis_index("row")
    col_id = lax.axis_index("col")
    row_count = lax.axis_size("row")
    col_count = lax.axis_size("col")
    leaf_count = lax.axis_size("leaf")
    half_id = leaf_id % 2
    ids = jnp.stack([half_id, row_id, col_id]).astype(jnp.int32)
    own_map = lax.dynamic_index_in_dim(block_map, leaf_id, 0, keepdims=False)
    partner_map = lax.dynamic_index_in_dim(block_map, leaf_id ^ 1, 0, keepdims=False)
    count = own_map.shape[0]

    child_block = child_front[0]
    child_rows, child_cols = child_block.shape
    width = child_cols // 2
    parent_rows, parent_cols = parent_front.shape
    row_span, col_span = parent_rows // BLK, parent_cols // BLK
    row_blocks, col_blocks = child_rows // BLK, child_cols // BLK
    first = width // BLK
    cap = -(-count // row_count)
    swap = [(i, i ^ 1) for i in range(leaf_count)]

    def only(axis, got, value, targets):
        index = lax.axis_index(axis)
        hit = functools.reduce(jnp.logical_or, [index == t for t in targets])
        return jnp.where(hit, got, value)

    def after(value, earlier):
        return lax.optimization_barrier((value, earlier))[0]

    grid = row_count * col_count

    def panel_parts(diagonal, slab, top, leaves, paired):
        def down(value, pairs):
            moves = [
                (l * grid + r * col_count, l * grid + q * col_count)
                for l in leaves for r, q in pairs
            ]
            return send(value, ("leaf", "row", "col"), moves)

        def along(value, pairs):
            moves = [(l * col_count + r, l * col_count + q) for l in leaves for r, q in pairs]
            got = send(value, ("leaf", "col"), moves)
            return only("col", got, value, [q for _, q in pairs])

        def over(value, pairs):
            return send(value, "row", pairs)

        def joined(value, bit):
            got = over(value, [(r, r ^ bit) for r in range(row_count)])
            upper = (row_id // bit) % 2 == 1
            return jnp.concatenate(
                [jnp.where(upper, got, value), jnp.where(upper, value, got)], axis=0
            )

        fan = list(range(2, row_count, 2))
        d1 = functools.reduce(jnp.add, [down(diagonal, [(0, q)]) for q in fan])
        d1 = only("row", d1, diagonal, fan)
        slab1 = along(slab, HALVING[0])
        size = top.shape[0] // 2
        half = only("row", over(top[size:], [(0, 4)]), top[:size], [4])
        zhi = [(r, r + 1) for r in range(0, row_count, 2)]
        d1 = after(d1, half if paired else (slab1, half))
        d2 = only("row", down(d1, zhi), d1, [q for _, q in zhi])
        half = only("row", over(after(half, d1), [(0, 1), (4, 5)]), half, [1, 5])
        if paired:
            d2 = after(d2, half)
        d3 = along(d2, HALVING[0])
        slab2 = along(after(slab1, d2), HALVING[1])
        copies = [(0, 2), (1, 3), (4, 6), (5, 7)]
        half = only("row", over(after(half, d2), copies), half, [q for _, q in copies])
        if paired:
            d3 = after(d3, half)
        d4 = along(d3, HALVING[1])
        slab3 = along(after(slab2, d4 if paired else d3), HALVING[2])
        top3 = joined(after(half, d3), 4)
        d5 = along(d4, HALVING[2])
        if paired:
            across = [(l, l + 1) for l in leaves]
            d5 = jnp.where(half_id == 0, d5, send(d5, "leaf", across))
            slab3 = after(slab3, d5)
            slab3 = jnp.where(half_id == 0, slab3, send(slab3, "leaf", across))
        return d5, slab3, top3

    diagonal, slab, top = panel_parts(
        child_block[:width, :width], child_block[:, :width], child_block[:width],
        list(range(leaf_count)), False,
    )
    inverse = inverse_factor(diagonal)
    rows_factor = lax.dot_general(slab, inverse, (((1,), (1,)), ((), ())), precision=HIGHEST)
    cols_factor = jnp.dot(inverse, top, precision=HIGHEST)
    contribution = child_block - jnp.dot(rows_factor, cols_factor, precision=HIGHEST)
    out_width = width // col_count
    child_out = lax.dynamic_slice_in_dim(rows_factor, col_id * out_width, out_width, 1).T

    strips = kernel_call(
        functools.partial(strips_kernel, (row_span, first, row_blocks)),
        "strips", (row_count, BLK, child_cols), 2, 1,
    )(ids, own_map, contribution)
    got = lax.all_to_all(strips, "row", 0, 0, tiled=True)
    tables = [pltpu.SMEM((count,), jnp.int32), pltpu.SMEM((cap,), jnp.int32)]
    tiles = kernel_call(
        functools.partial(
            tiles_kernel,
            (row_span, col_span, first, row_blocks, col_blocks, col_count, count),
        ),
        "tiles", (col_count, cap, BLK, BLK), 2, 1, tables,
    )(ids, own_map, got)
    landed = lax.all_to_all(
        tiles.reshape(col_count, cap * BLK, BLK), "col", 0, 0, tiled=True
    ).reshape(tiles.shape)
    other = kernel_call(
        functools.partial(other_kernel, (col_span, first, col_blocks, col_count, count)),
        "other", (col_span, cap, BLK, BLK), 2, 1,
    )(ids, own_map, landed)
    other = send(other, "leaf", swap)

    parent_order = parent_rows * row_count
    parent_width = parent_cols // 2
    assembled, diagonal, slab, top = kernel_call(
        functools.partial(
            assemble_kernel, (row_span, col_span, first, col_blocks, col_count, count)
        ),
        "assemble",
        [
            parent_front.shape, (parent_width, parent_width),
            (parent_rows, parent_width), (parent_width, parent_cols),
        ],
        3, 3, tables + [pltpu.SMEM((cap,), jnp.int32)],
    )(ids, own_map, partner_map, parent_front, other, landed)
    diagonal, slab, top = panel_parts(
        diagonal, slab, top, list(range(0, leaf_count, 2)), True
    )
    inverse = inverse_factor(diagonal)
    rows_factor = lax.dot_general(slab, inverse, (((1,), (1,)), ((), ())), precision=HIGHEST)
    cols_factor = jnp.dot(inverse, top, precision=HIGHEST)
    update = jnp.dot(rows_factor, cols_factor, precision=HIGHEST)
    row_ids = row_id * parent_rows + jnp.arange(parent_rows)
    col_ids = half_id * (parent_order // 2) + col_id * parent_cols + jnp.arange(parent_cols)
    keep = (row_ids[:, None] >= parent_width) & (col_ids[None, :] >= parent_width)
    parent_schur = jnp.where(keep, assembled - update, jnp.float32(0.0))
    share = parent_width // (2 * col_count)
    start = (half_id * col_count + col_id) * share
    parent_out = lax.dynamic_slice_in_dim(rows_factor, start, share, 1).T
    return (child_out[None], parent_out, parent_schur)


def solution(mesh):
    placed = (P("leaf", "row", "col"), P("row", ("leaf", "col")), P())
    return jax.shard_map(
        shards,
        mesh=mesh,
        in_specs=placed,
        out_specs=(P("leaf", "col", "row"), P(("leaf", "col"), "row"), P("row", ("leaf", "col"))),
        check_vma=False,
    )
```

```python
import functools

import jax
import jax.numpy as jnp
from jax import lax
from jax.experimental import pallas as pl
from jax.experimental.pallas import tpu as pltpu
from jax.sharding import PartitionSpec as P

BLK = 128
STEP = 64
GROUP = 8
HIGHEST = lax.Precision.HIGHEST


def send(value, axes, pairs):
    return lax.ppermute(value, axes, pairs)


HALVING = ([(0, 4)], [(0, 2), (4, 6)], [(0, 1), (2, 3), (4, 5), (6, 7)])


def reciprocal(x):
    guess = pltpu.reciprocal(x, approx=True)
    guess = guess * (2.0 - x * guess)
    return guess * (2.0 - x * guess)


def inverse_factor_kernel(a_ref, out_ref, x_ref):
    order = a_ref.shape[0]
    f32 = jnp.float32
    value = a_ref[...]
    full_sub = lax.broadcasted_iota(jnp.int32, value.shape, 0)
    full_lane = lax.broadcasted_iota(jnp.int32, value.shape, 1)
    diagonal = jnp.where(full_sub == full_lane, value, 0.0)
    scale_col = lax.rsqrt(jnp.sum(diagonal, axis=1, keepdims=True))
    scale_row = lax.rsqrt(jnp.sum(diagonal, axis=0, keepdims=True))
    x_ref[...] = (value * scale_col) * scale_row
    wide = (STEP, 2 * STEP)
    sub = lax.broadcasted_iota(jnp.int32, wide, 0)
    lane = lax.broadcasted_iota(jnp.int32, wide, 1)
    eye = (sub[:, :STEP] == lane[:, :STEP]).astype(f32)
    for start in range(0, order, STEP):
        stop = start + STEP
        rows = x_ref[start:stop, :]
        work = jnp.concatenate([x_ref[start:stop, start:stop], eye], axis=1)
        for base in range(0, STEP, GROUP):
            cols = [
                jnp.broadcast_to(work[:, base + j : base + j + 1], wide) for j in range(GROUP)
            ]
            for j in range(0, GROUP, 2):
                k = base + j
                c0, c1 = cols[j], cols[j + 1]
                p00, p01, p11 = c0[k : k + 1], c1[k : k + 1], c1[k + 1 : k + 2]
                over = reciprocal(p00 * p11 - p01 * p01)
                a00, a01, a11 = p00 * over, p01 * over, p11 * over
                below = sub > k + 1
                f0 = jnp.where(below, c0 * a11 - c1 * a01, 0.0)
                f1 = jnp.where(below, c1 * a00 - c0 * a01, 0.0)
                for i in range(j + 2, GROUP):
                    cols[i] = cols[i] - f0 * cols[i][k : k + 1] - f1 * cols[i][k + 1 : k + 2]
                work = work - f0 * work[k : k + 1] - f1 * work[k + 1 : k + 2]
        pivots = jnp.sum(jnp.where(sub == lane, work, 0.0), axis=1, keepdims=True)
        left = jnp.sum(jnp.where(sub == lane + 1, work, 0.0), axis=1, keepdims=True)
        above = pltpu.roll(jnp.broadcast_to(pivots, wide), 1, 0)
        work = work - jnp.where(sub % 2 == 1, left / above, 0.0) * pltpu.roll(work, 1, 0)
        pivots = jnp.sum(jnp.where(sub == lane, work, 0.0), axis=1, keepdims=True)
        inverse = work[:, STEP:] * lax.rsqrt(pivots)
        panel = jnp.dot(inverse, rows, precision=HIGHEST, preferred_element_type=f32)
        pieces = [inverse]
        if start:
            pieces.insert(0, panel[:, :start])
        if stop < order:
            pieces.append(panel[:, stop:])
        panel = jnp.concatenate(pieces, axis=1)
        x_ref[start:stop, :] = panel
        if stop < order:
            change = lax.dot_general(
                panel[:, stop:], panel, (((0,), (0,)), ((), ())),
                precision=HIGHEST, preferred_element_type=f32,
            )
            old = x_ref[stop:, :]
            at = lax.broadcasted_iota(jnp.int32, old.shape, 1)
            x_ref[stop:, :] = jnp.where((at >= start) & (at < stop), 0.0, old) - change
    out_ref[...] = jnp.where(full_lane <= full_sub, x_ref[...] * scale_row, 0.0)


def inverse_factor(block):
    return pl.pallas_call(
        inverse_factor_kernel,
        out_shape=jax.ShapeDtypeStruct(block.shape, jnp.float32),
        scratch_shapes=[pltpu.VMEM(block.shape, jnp.float32)],
        name="inverse_factor",
    )(block)


def smem():
    return pl.BlockSpec(memory_space=pltpu.SMEM)


def vmem():
    return pl.BlockSpec(memory_space=pltpu.VMEM)


def row_tables(map_ref, row, row_span, count, rank_ref, at_ref):
    for m in range(at_ref.shape[0]):
        at_ref[m] = -1

    def body(k, rank):
        here = map_ref[k] // row_span == row
        rank_ref[k] = jnp.where(here, rank, -1)

        @pl.when(here)
        def _():
            at_ref[jnp.minimum(rank, at_ref.shape[0] - 1)] = map_ref[k] % row_span

        return rank + here.astype(jnp.int32)

    lax.fori_loop(0, count, body, jnp.int32(0))


def strips_kernel(sizes, ids_ref, map_ref, part_ref, out_ref):
    row_span, first, row_blocks = sizes
    row = ids_ref[1]
    for a in range(row_blocks):
        block = row * row_blocks + a - first

        @pl.when(block >= 0)
        def _():
            target = map_ref[jnp.maximum(block, 0)] // row_span
            out_ref[target] = part_ref[a * BLK : (a + 1) * BLK, :]


def tiles_kernel(sizes, ids_ref, map_ref, got_ref, out_ref, rank_ref, at_ref):
    row_span, col_span, first, row_blocks, col_blocks, cols, count = sizes
    row, col = ids_ref[1], ids_ref[2]
    row_tables(map_ref, row, row_span, count, rank_ref, at_ref)

    def body(k, carry):
        rank = rank_ref[k]

        @pl.when(rank >= 0)
        def _():
            source = (k + first) // row_blocks
            slot = jnp.minimum(rank, out_ref.shape[1] - 1)
            for y in range(col_blocks):
                block = col * col_blocks + y - first

                @pl.when(block >= 0)
                def _():
                    target = (map_ref[jnp.maximum(block, 0)] // col_span) % cols
                    out_ref[target, slot] = got_ref[source, :, y * BLK : (y + 1) * BLK]

        return carry

    lax.fori_loop(0, count, body, jnp.int32(0))


def other_kernel(sizes, ids_ref, map_ref, landed_ref, out_ref):
    col_span, first, col_blocks, cols, count = sizes
    half, col = ids_ref[0], ids_ref[2]
    out_ref[...] = jnp.zeros_like(out_ref)

    def body(k, carry):
        owner = map_ref[k] // col_span

        @pl.when((owner % cols == col) & (owner // cols != half))
        def _():
            out_ref[map_ref[k] % col_span] = landed_ref[(k + first) // col_blocks]

        return carry

    lax.fori_loop(0, count, body, jnp.int32(0))


def assemble_kernel(sizes, ids_ref, map_ref, pair_map_ref, parent_ref, other_ref, landed_ref,
                    out_ref, diagonal_ref, slab_ref, top_ref, rank_ref, at_ref, pair_at_ref):
    row_span, col_span, first, col_blocks, cols, count = sizes
    half, row, col = ids_ref[0], ids_ref[1], ids_ref[2]
    out_ref[...] = parent_ref[...].astype(jnp.float32)
    row_tables(pair_map_ref, row, row_span, count, rank_ref, pair_at_ref)
    row_tables(map_ref, row, row_span, count, rank_ref, at_ref)
    caps = at_ref.shape[0]
    for m in range(caps):
        at = pair_at_ref[m]

        @pl.when(at >= 0)
        def _():
            for y in range(col_span):
                spot = (
                    pl.ds(pl.multiple_of(at * BLK, BLK), BLK), slice(y * BLK, (y + 1) * BLK)
                )
                out_ref[spot] = out_ref[spot] + other_ref[y, m]

    def body(k, carry):
        owner = map_ref[k] // col_span

        @pl.when((owner % cols == col) & (owner // cols == half))
        def _():
            at_col = pl.ds(pl.multiple_of((map_ref[k] % col_span) * BLK, BLK), BLK)
            for m in range(caps):
                at = at_ref[m]

                @pl.when(at >= 0)
                def _():
                    spot = (pl.ds(pl.multiple_of(at * BLK, BLK), BLK), at_col)
                    out_ref[spot] = out_ref[spot] + landed_ref[(k + first) // col_blocks, m]

        return carry

    lax.fori_loop(0, count, body, jnp.int32(0))
    width = diagonal_ref.shape[0]
    diagonal_ref[...] = out_ref[:width, :width]
    slab_ref[...] = out_ref[:, :width]
    top_ref[...] = out_ref[:width, :]


def kernel_call(body, name, outs, n_smem, n_vmem, scratch=()):
    many = isinstance(outs, list)
    shapes = [jax.ShapeDtypeStruct(o, jnp.float32) for o in (outs if many else [outs])]
    specs = [vmem() for _ in shapes]
    return pl.pallas_call(
        body,
        out_shape=shapes if many else shapes[0],
        in_specs=[smem()] * n_smem + [vmem()] * n_vmem,
        out_specs=specs if many else specs[0],
        scratch_shapes=list(scratch),
        compiler_params=pltpu.CompilerParams(vmem_limit_bytes=40 * 2**20),
        name=name,
    )


def shards(child_front, parent_front, block_map):
    leaf_id = lax.axis_index("leaf")
    row_id = lax.axis_index("row")
    col_id = lax.axis_index("col")
    row_count = lax.axis_size("row")
    col_count = lax.axis_size("col")
    leaf_count = lax.axis_size("leaf")
    half_id = leaf_id % 2
    ids = jnp.stack([half_id, row_id, col_id]).astype(jnp.int32)
    own_map = lax.dynamic_index_in_dim(block_map, leaf_id, 0, keepdims=False)
    partner_map = lax.dynamic_index_in_dim(block_map, leaf_id ^ 1, 0, keepdims=False)
    count = own_map.shape[0]

    child_block = child_front[0]
    child_rows, child_cols = child_block.shape
    width = child_cols // 2
    parent_rows, parent_cols = parent_front.shape
    row_span, col_span = parent_rows // BLK, parent_cols // BLK
    row_blocks, col_blocks = child_rows // BLK, child_cols // BLK
    first = width // BLK
    cap = -(-count // row_count)
    swap = [(i, i ^ 1) for i in range(leaf_count)]

    def only(axis, got, value, targets):
        index = lax.axis_index(axis)
        hit = functools.reduce(jnp.logical_or, [index == t for t in targets])
        return jnp.where(hit, got, value)

    def after(value, earlier):
        return lax.optimization_barrier((value, earlier))[0]

    grid = row_count * col_count

    def panel_parts(diagonal, slab, top, leaves, paired):
        def down(value, pairs):
            moves = [
                (l * grid + r * col_count, l * grid + q * col_count)
                for l in leaves for r, q in pairs
            ]
            return send(value, ("leaf", "row", "col"), moves)

        def along(value, pairs):
            moves = [(l * col_count + r, l * col_count + q) for l in leaves for r, q in pairs]
            got = send(value, ("leaf", "col"), moves)
            return only("col", got, value, [q for _, q in pairs])

        def over(value, pairs):
            return send(value, "row", pairs)

        def joined(value, bit):
            got = over(value, [(r, r ^ bit) for r in range(row_count)])
            upper = (row_id // bit) % 2 == 1
            return jnp.concatenate(
                [jnp.where(upper, got, value), jnp.where(upper, value, got)], axis=0
            )

        fan = list(range(2, row_count, 2))
        d1 = functools.reduce(jnp.add, [down(diagonal, [(0, q)]) for q in fan])
        d1 = only("row", d1, diagonal, fan)
        slab1 = along(slab, HALVING[0])
        size = top.shape[0] // (row_count // 2)
        part = [over(top[q // 2 * size : (q // 2 + 1) * size], [(0, q)]) for q in fan]
        part = only("row", functools.reduce(jnp.add, part), top[:size], fan)
        zhi = [(r, r + 1) for r in range(0, row_count, 2)]
        d2 = only("row", down(d1, zhi), d1, [q for _, q in zhi])
        part = only("row", over(after(part, d1), zhi), part, [q for _, q in zhi])
        d3 = along(d2, HALVING[0])
        slab2 = along(after(slab1, d2), HALVING[1])
        part = joined(after(part, d2), 2)
        d4 = along(d3, HALVING[1])
        slab3 = along(after(slab2, d3), HALVING[2])
        top3 = joined(after(part, d3), 4)
        d5 = along(d4, HALVING[2])
        if paired:
            across = [(l, l + 1) for l in leaves]
            d5 = jnp.where(half_id == 0, d5, send(d5, "leaf", across))
            slab3 = jnp.where(half_id == 0, slab3, send(slab3, "leaf", across))
        return d5, slab3, top3

    diagonal, slab, top = panel_parts(
        child_block[:width, :width], child_block[:, :width], child_block[:width],
        list(range(leaf_count)), False,
    )
    inverse = inverse_factor(diagonal)
    rows_factor = lax.dot_general(slab, inverse, (((1,), (1,)), ((), ())), precision=HIGHEST)
    cols_factor = jnp.dot(inverse, top, precision=HIGHEST)
    contribution = child_block - jnp.dot(rows_factor, cols_factor, precision=HIGHEST)
    out_width = width // col_count
    child_out = lax.dynamic_slice_in_dim(rows_factor, col_id * out_width, out_width, 1).T

    strips = kernel_call(
        functools.partial(strips_kernel, (row_span, first, row_blocks)),
        "strips", (row_count, BLK, child_cols), 2, 1,
    )(ids, own_map, contribution)
    got = lax.all_to_all(strips, "row", 0, 0, tiled=True)
    tables = [pltpu.SMEM((count,), jnp.int32), pltpu.SMEM((cap,), jnp.int32)]
    tiles = kernel_call(
        functools.partial(
            tiles_kernel,
            (row_span, col_span, first, row_blocks, col_blocks, col_count, count),
        ),
        "tiles", (col_count, cap, BLK, BLK), 2, 1, tables,
    )(ids, own_map, got)
    landed = lax.all_to_all(
        tiles.reshape(col_count, cap * BLK, BLK), "col", 0, 0, tiled=True
    ).reshape(tiles.shape)
    other = kernel_call(
        functools.partial(other_kernel, (col_span, first, col_blocks, col_count, count)),
        "other", (col_span, cap, BLK, BLK), 2, 1,
    )(ids, own_map, landed)
    other = send(other, "leaf", swap)

    parent_order = parent_rows * row_count
    parent_width = parent_cols // 2
    assembled, diagonal, slab, top = kernel_call(
        functools.partial(
            assemble_kernel, (row_span, col_span, first, col_blocks, col_count, count)
        ),
        "assemble",
        [
            parent_front.shape, (parent_width, parent_width),
            (parent_rows, parent_width), (parent_width, parent_cols),
        ],
        3, 3, tables + [pltpu.SMEM((cap,), jnp.int32)],
    )(ids, own_map, partner_map, parent_front, other, landed)
    diagonal, slab, top = panel_parts(
        diagonal, slab, top, list(range(0, leaf_count, 2)), True
    )
    inverse = inverse_factor(diagonal)
    rows_factor = lax.dot_general(slab, inverse, (((1,), (1,)), ((), ())), precision=HIGHEST)
    cols_factor = jnp.dot(inverse, top, precision=HIGHEST)
    update = jnp.dot(rows_factor, cols_factor, precision=HIGHEST)
    row_ids = row_id * parent_rows + jnp.arange(parent_rows)
    col_ids = half_id * (parent_order // 2) + col_id * parent_cols + jnp.arange(parent_cols)
    keep = (row_ids[:, None] >= parent_width) & (col_ids[None, :] >= parent_width)
    parent_schur = jnp.where(keep, assembled - update, jnp.float32(0.0))
    share = parent_width // (2 * col_count)
    start = (half_id * col_count + col_id) * share
    parent_out = lax.dynamic_slice_in_dim(rows_factor, start, share, 1).T
    return (child_out[None], parent_out, parent_schur)


def solution(mesh):
    placed = (P("leaf", "row", "col"), P("row", ("leaf", "col")), P())
    return jax.shard_map(
        shards,
        mesh=mesh,
        in_specs=placed,
        out_specs=(P("leaf", "col", "row"), P(("leaf", "col"), "row"), P("row", ("leaf", "col"))),
        check_vma=False,
    )
```

```python
import functools

import jax
import jax.numpy as jnp
from jax import lax
from jax.experimental import pallas as pl
from jax.experimental.pallas import tpu as pltpu
from jax.sharding import PartitionSpec as P

BLK = 128
STEP = 64
GROUP = 8
HIGHEST = lax.Precision.HIGHEST


def send(value, axes, pairs):
    return lax.ppermute(value, axes, pairs)


HALVING = ([(0, 4)], [(0, 2), (4, 6)], [(0, 1), (2, 3), (4, 5), (6, 7)])


def reciprocal(x):
    guess = pltpu.reciprocal(x, approx=True)
    guess = guess * (2.0 - x * guess)
    return guess * (2.0 - x * guess)


def inverse_factor_kernel(a_ref, out_ref, x_ref):
    order = a_ref.shape[0]
    f32 = jnp.float32
    value = a_ref[...]
    full_sub = lax.broadcasted_iota(jnp.int32, value.shape, 0)
    full_lane = lax.broadcasted_iota(jnp.int32, value.shape, 1)
    diagonal = jnp.where(full_sub == full_lane, value, 0.0)
    scale_col = lax.rsqrt(jnp.sum(diagonal, axis=1, keepdims=True))
    scale_row = lax.rsqrt(jnp.sum(diagonal, axis=0, keepdims=True))
    x_ref[...] = (value * scale_col) * scale_row
    wide = (STEP, 2 * STEP)
    sub = lax.broadcasted_iota(jnp.int32, wide, 0)
    lane = lax.broadcasted_iota(jnp.int32, wide, 1)
    eye = (sub[:, :STEP] == lane[:, :STEP]).astype(f32)
    for start in range(0, order, STEP):
        stop = start + STEP
        rows = x_ref[start:stop, :]
        work = jnp.concatenate([x_ref[start:stop, start:stop], eye], axis=1)
        for base in range(0, STEP, GROUP):
            cols = [
                jnp.broadcast_to(work[:, base + j : base + j + 1], wide) for j in range(GROUP)
            ]
            for j in range(0, GROUP, 2):
                k = base + j
                c0, c1 = cols[j], cols[j + 1]
                p00, p01, p11 = c0[k : k + 1], c1[k : k + 1], c1[k + 1 : k + 2]
                over = reciprocal(p00 * p11 - p01 * p01)
                a00, a01, a11 = p00 * over, p01 * over, p11 * over
                below = sub > k + 1
                f0 = jnp.where(below, c0 * a11 - c1 * a01, 0.0)
                f1 = jnp.where(below, c1 * a00 - c0 * a01, 0.0)
                for i in range(j + 2, GROUP):
                    cols[i] = cols[i] - f0 * cols[i][k : k + 1] - f1 * cols[i][k + 1 : k + 2]
                work = work - f0 * work[k : k + 1] - f1 * work[k + 1 : k + 2]
        pivots = jnp.sum(jnp.where(sub == lane, work, 0.0), axis=1, keepdims=True)
        left = jnp.sum(jnp.where(sub == lane + 1, work, 0.0), axis=1, keepdims=True)
        above = pltpu.roll(jnp.broadcast_to(pivots, wide), 1, 0)
        work = work - jnp.where(sub % 2 == 1, left / above, 0.0) * pltpu.roll(work, 1, 0)
        pivots = jnp.sum(jnp.where(sub == lane, work, 0.0), axis=1, keepdims=True)
        inverse = work[:, STEP:] * lax.rsqrt(pivots)
        panel = jnp.dot(inverse, rows, precision=HIGHEST, preferred_element_type=f32)
        pieces = [inverse]
        if start:
            pieces.insert(0, panel[:, :start])
        if stop < order:
            pieces.append(panel[:, stop:])
        panel = jnp.concatenate(pieces, axis=1)
        x_ref[start:stop, :] = panel
        if stop < order:
            change = lax.dot_general(
                panel[:, stop:], panel, (((0,), (0,)), ((), ())),
                precision=HIGHEST, preferred_element_type=f32,
            )
            old = x_ref[stop:, :]
            at = lax.broadcasted_iota(jnp.int32, old.shape, 1)
            x_ref[stop:, :] = jnp.where((at >= start) & (at < stop), 0.0, old) - change
    out_ref[...] = jnp.where(full_lane <= full_sub, x_ref[...] * scale_row, 0.0)


def inverse_factor(block):
    return pl.pallas_call(
        inverse_factor_kernel,
        out_shape=jax.ShapeDtypeStruct(block.shape, jnp.float32),
        scratch_shapes=[pltpu.VMEM(block.shape, jnp.float32)],
        name="inverse_factor",
    )(block)


def smem():
    return pl.BlockSpec(memory_space=pltpu.SMEM)


def vmem():
    return pl.BlockSpec(memory_space=pltpu.VMEM)


def row_tables(map_ref, row, row_span, count, rank_ref, at_ref):
    for m in range(at_ref.shape[0]):
        at_ref[m] = -1

    def body(k, rank):
        here = map_ref[k] // row_span == row
        rank_ref[k] = jnp.where(here, rank, -1)

        @pl.when(here)
        def _():
            at_ref[jnp.minimum(rank, at_ref.shape[0] - 1)] = map_ref[k] % row_span

        return rank + here.astype(jnp.int32)

    lax.fori_loop(0, count, body, jnp.int32(0))


def strips_kernel(sizes, ids_ref, map_ref, part_ref, out_ref):
    row_span, first, row_blocks = sizes
    row = ids_ref[1]
    for a in range(row_blocks):
        block = row * row_blocks + a - first

        @pl.when(block >= 0)
        def _():
            target = map_ref[jnp.maximum(block, 0)] // row_span
            out_ref[target] = part_ref[a * BLK : (a + 1) * BLK, :]


def tiles_kernel(sizes, ids_ref, map_ref, got_ref, out_ref, rank_ref, at_ref):
    row_span, col_span, first, row_blocks, col_blocks, cols, count = sizes
    row, col = ids_ref[1], ids_ref[2]
    row_tables(map_ref, row, row_span, count, rank_ref, at_ref)

    def body(k, carry):
        rank = rank_ref[k]

        @pl.when(rank >= 0)
        def _():
            source = (k + first) // row_blocks
            slot = jnp.minimum(rank, out_ref.shape[1] - 1)
            for y in range(col_blocks):
                block = col * col_blocks + y - first

                @pl.when(block >= 0)
                def _():
                    target = (map_ref[jnp.maximum(block, 0)] // col_span) % cols
                    out_ref[target, slot] = got_ref[source, :, y * BLK : (y + 1) * BLK]

        return carry

    lax.fori_loop(0, count, body, jnp.int32(0))


def other_kernel(sizes, ids_ref, map_ref, landed_ref, out_ref):
    col_span, first, col_blocks, cols, count = sizes
    half, col = ids_ref[0], ids_ref[2]
    out_ref[...] = jnp.zeros_like(out_ref)

    def body(k, carry):
        owner = map_ref[k] // col_span

        @pl.when((owner % cols == col) & (owner // cols != half))
        def _():
            out_ref[map_ref[k] % col_span] = landed_ref[(k + first) // col_blocks]

        return carry

    lax.fori_loop(0, count, body, jnp.int32(0))


def assemble_kernel(sizes, ids_ref, map_ref, pair_map_ref, parent_ref, other_ref, landed_ref,
                    out_ref, diagonal_ref, slab_ref, top_ref, rank_ref, at_ref, pair_at_ref):
    row_span, col_span, first, col_blocks, cols, count = sizes
    half, row, col = ids_ref[0], ids_ref[1], ids_ref[2]
    out_ref[...] = parent_ref[...].astype(jnp.float32)
    row_tables(pair_map_ref, row, row_span, count, rank_ref, pair_at_ref)
    row_tables(map_ref, row, row_span, count, rank_ref, at_ref)
    caps = at_ref.shape[0]
    for m in range(caps):
        at = pair_at_ref[m]

        @pl.when(at >= 0)
        def _():
            for y in range(col_span):
                spot = (
                    pl.ds(pl.multiple_of(at * BLK, BLK), BLK), slice(y * BLK, (y + 1) * BLK)
                )
                out_ref[spot] = out_ref[spot] + other_ref[y, m]

    def body(k, carry):
        owner = map_ref[k] // col_span

        @pl.when((owner % cols == col) & (owner // cols == half))
        def _():
            at_col = pl.ds(pl.multiple_of((map_ref[k] % col_span) * BLK, BLK), BLK)
            for m in range(caps):
                at = at_ref[m]

                @pl.when(at >= 0)
                def _():
                    spot = (pl.ds(pl.multiple_of(at * BLK, BLK), BLK), at_col)
                    out_ref[spot] = out_ref[spot] + landed_ref[(k + first) // col_blocks, m]

        return carry

    lax.fori_loop(0, count, body, jnp.int32(0))
    width = diagonal_ref.shape[0]
    diagonal_ref[...] = out_ref[:width, :width]
    slab_ref[...] = out_ref[:, :width]
    top_ref[...] = out_ref[:width, :]


def kernel_call(body, name, outs, n_smem, n_vmem, scratch=()):
    many = isinstance(outs, list)
    shapes = [jax.ShapeDtypeStruct(o, jnp.float32) for o in (outs if many else [outs])]
    specs = [vmem() for _ in shapes]
    return pl.pallas_call(
        body,
        out_shape=shapes if many else shapes[0],
        in_specs=[smem()] * n_smem + [vmem()] * n_vmem,
        out_specs=specs if many else specs[0],
        scratch_shapes=list(scratch),
        compiler_params=pltpu.CompilerParams(vmem_limit_bytes=40 * 2**20),
        name=name,
    )


def shards(child_front, parent_front, block_map):
    leaf_id = lax.axis_index("leaf")
    row_id = lax.axis_index("row")
    col_id = lax.axis_index("col")
    row_count = lax.axis_size("row")
    col_count = lax.axis_size("col")
    leaf_count = lax.axis_size("leaf")
    half_id = leaf_id % 2
    ids = jnp.stack([half_id, row_id, col_id]).astype(jnp.int32)
    own_map = lax.dynamic_index_in_dim(block_map, leaf_id, 0, keepdims=False)
    partner_map = lax.dynamic_index_in_dim(block_map, leaf_id ^ 1, 0, keepdims=False)
    count = own_map.shape[0]

    child_block = child_front[0]
    child_rows, child_cols = child_block.shape
    width = child_cols // 2
    parent_rows, parent_cols = parent_front.shape
    row_span, col_span = parent_rows // BLK, parent_cols // BLK
    row_blocks, col_blocks = child_rows // BLK, child_cols // BLK
    first = width // BLK
    cap = -(-count // row_count)
    swap = [(i, i ^ 1) for i in range(leaf_count)]

    def only(axis, got, value, targets):
        index = lax.axis_index(axis)
        hit = functools.reduce(jnp.logical_or, [index == t for t in targets])
        return jnp.where(hit, got, value)

    def after(value, earlier):
        return lax.optimization_barrier((value, earlier))[0]

    grid = row_count * col_count

    def panel_parts(diagonal, slab, top, leaves, paired):
        def down(value, pairs):
            moves = [
                (l * grid + r * col_count, l * grid + q * col_count)
                for l in leaves for r, q in pairs
            ]
            return send(value, ("leaf", "row", "col"), moves)

        def along(value, pairs):
            moves = [(l * col_count + r, l * col_count + q) for l in leaves for r, q in pairs]
            got = send(value, ("leaf", "col"), moves)
            return only("col", got, value, [q for _, q in pairs])

        def over(value, pairs):
            return send(value, "row", pairs)

        def joined(value, bit):
            got = over(value, [(r, r ^ bit) for r in range(row_count)])
            upper = (row_id // bit) % 2 == 1
            return jnp.concatenate(
                [jnp.where(upper, got, value), jnp.where(upper, value, got)], axis=0
            )

        fan = list(range(2, row_count, 2))
        d1 = functools.reduce(jnp.add, [down(diagonal, [(0, q)]) for q in fan])
        d1 = only("row", d1, diagonal, fan)
        slab1 = along(slab, HALVING[0])
        size = top.shape[0] // (row_count // 2)
        part = [over(top[q // 2 * size : (q // 2 + 1) * size], [(0, q)]) for q in fan]
        part = only("row", functools.reduce(jnp.add, part), top[:size], fan)
        zhi = [(r, r + 1) for r in range(0, row_count, 2)]
        if paired:
            d1 = after(d1, part)
        d2 = only("row", down(d1, zhi), d1, [q for _, q in zhi])
        part = only("row", over(after(part, d1), zhi), part, [q for _, q in zhi])
        d3 = along(d2, HALVING[0])
        slab2 = along(after(slab1, d2), HALVING[1])
        part = joined(after(part, d2), 2)
        d4 = along(d3, HALVING[1])
        slab3 = along(after(slab2, d3), HALVING[2])
        top3 = joined(after(part, d3), 4)
        d5 = along(d4, HALVING[2])
        if paired:
            across = [(l, l + 1) for l in leaves]
            d5 = jnp.where(half_id == 0, d5, send(d5, "leaf", across))
            slab3 = jnp.where(half_id == 0, slab3, send(slab3, "leaf", across))
        return d5, slab3, top3

    diagonal, slab, top = panel_parts(
        child_block[:width, :width], child_block[:, :width], child_block[:width],
        list(range(leaf_count)), False,
    )
    inverse = inverse_factor(diagonal)
    rows_factor = lax.dot_general(slab, inverse, (((1,), (1,)), ((), ())), precision=HIGHEST)
    cols_factor = jnp.dot(inverse, top, precision=HIGHEST)
    contribution = child_block - jnp.dot(rows_factor, cols_factor, precision=HIGHEST)
    out_width = width // col_count
    child_out = lax.dynamic_slice_in_dim(rows_factor, col_id * out_width, out_width, 1).T

    strips = kernel_call(
        functools.partial(strips_kernel, (row_span, first, row_blocks)),
        "strips", (row_count, BLK, child_cols), 2, 1,
    )(ids, own_map, contribution)
    got = lax.all_to_all(strips, "row", 0, 0, tiled=True)
    tables = [pltpu.SMEM((count,), jnp.int32), pltpu.SMEM((cap,), jnp.int32)]
    tiles = kernel_call(
        functools.partial(
            tiles_kernel,
            (row_span, col_span, first, row_blocks, col_blocks, col_count, count),
        ),
        "tiles", (col_count, cap, BLK, BLK), 2, 1, tables,
    )(ids, own_map, got)
    landed = lax.all_to_all(
        tiles.reshape(col_count, cap * BLK, BLK), "col", 0, 0, tiled=True
    ).reshape(tiles.shape)
    other = kernel_call(
        functools.partial(other_kernel, (col_span, first, col_blocks, col_count, count)),
        "other", (col_span, cap, BLK, BLK), 2, 1,
    )(ids, own_map, landed)
    other = send(other, "leaf", swap)

    parent_order = parent_rows * row_count
    parent_width = parent_cols // 2
    assembled, diagonal, slab, top = kernel_call(
        functools.partial(
            assemble_kernel, (row_span, col_span, first, col_blocks, col_count, count)
        ),
        "assemble",
        [
            parent_front.shape, (parent_width, parent_width),
            (parent_rows, parent_width), (parent_width, parent_cols),
        ],
        3, 3, tables + [pltpu.SMEM((cap,), jnp.int32)],
    )(ids, own_map, partner_map, parent_front, other, landed)
    diagonal, slab, top = panel_parts(
        diagonal, slab, top, list(range(0, leaf_count, 2)), True
    )
    inverse = inverse_factor(diagonal)
    rows_factor = lax.dot_general(slab, inverse, (((1,), (1,)), ((), ())), precision=HIGHEST)
    cols_factor = jnp.dot(inverse, top, precision=HIGHEST)
    update = jnp.dot(rows_factor, cols_factor, precision=HIGHEST)
    row_ids = row_id * parent_rows + jnp.arange(parent_rows)
    col_ids = half_id * (parent_order // 2) + col_id * parent_cols + jnp.arange(parent_cols)
    keep = (row_ids[:, None] >= parent_width) & (col_ids[None, :] >= parent_width)
    parent_schur = jnp.where(keep, assembled - update, jnp.float32(0.0))
    share = parent_width // (2 * col_count)
    start = (half_id * col_count + col_id) * share
    parent_out = lax.dynamic_slice_in_dim(rows_factor, start, share, 1).T
    return (child_out[None], parent_out, parent_schur)


def solution(mesh):
    placed = (P("leaf", "row", "col"), P("row", ("leaf", "col")), P())
    return jax.shard_map(
        shards,
        mesh=mesh,
        in_specs=placed,
        out_specs=(P("leaf", "col", "row"), P(("leaf", "col"), "row"), P("row", ("leaf", "col"))),
        check_vma=False,
    )
```
